256 devices in a mesh: seq: 32 (over y_lo, z, core), fsdp: 8 (over y_hi, x).
Axes of the slice: x: 4, y: 4 (y_hi: 2, y_lo: 2; y = y_hi * 2 + y_lo), z: 8, core: 2. Of those that a mesh axis runs over, the one named last changes fastest.
Arguments:
- tokens: bfloat16 [8, 32768, 1024], P('fsdp', 'seq'), may hold values from -6 to 6
- qkv_base: bfloat16 [1024, 3072], P('fsdp'), may hold values from -1 to 1
- qkv_dir: bfloat16 [1024, 3072], P('fsdp'), may hold values from -0.1875 to 0.1875
- out_base: bfloat16 [1024, 1024], P('fsdp'), may hold values from -0.1875 to 0.1875
- out_dir: bfloat16 [1024, 1024], P('fsdp'), may hold values from -0.1875 to 0.1875
- alpha_index: int32 [1], replicated, may hold values from 0 to 1023
Outputs:
- attn_delta: bfloat16 [8, 32768, 1024], P('fsdp', 'seq')
The draws below stay inside these ranges and needn't reach their ends.
All inputs are finite; a program needn't handle non-finite values.
Results may differ from the reference program's by a relative error of at most 0.011.
Values may be sent and summed in bfloat16 or wider, within the bound.
No kernel may reach another device: no remote copies, remote signals or barrier semaphores. Data moves between devices by JAX's collectives and lax.ppermute only.
A program may use at most 192 MiB of HBM per device.

```python
import math
import jax
import jax.numpy as jnp
from jax import lax

D = 1024
HEADS = 16
STRIDE = 1024
NALPHA = 1024
SEQ_LEN = 32768
BATCH = 8


def draw_qkv_base(key, part):
    first_key = jax.random.fold_in(jax.random.fold_in(key, 11), 0)
    return jnp.clip(jax.random.normal(first_key, (D, 3 * D), jnp.float32) / math.sqrt(D), -1.0, 1.0).astype(jnp.bfloat16)


def block_scale(own_key, dims, cuts, least, largest):
    def one(dim, shards_of):
        heights = jax.random.uniform(jax.random.fold_in(jax.random.fold_in(own_key, 6), dim), (shards_of,), jnp.float32, least / len(cuts), largest / len(cuts))
        return jnp.repeat(jnp.exp(heights), dims[dim] // shards_of).reshape((-1,) + (1,) * (len(dims) - dim - 1))

    level = one(*cuts[0])
    for cut in cuts[1:]:
        level = level * one(*cut)
    return level


def gaussian(own_key, extent, deviation, bound, cuts=(), held_as=jnp.bfloat16):
    loudness = block_scale(own_key, extent, cuts, -0.22, 0.18) if cuts else 1.0
    drawn = jax.random.normal(own_key, extent, jnp.float32) * deviation * loudness
    return jnp.minimum(jnp.maximum(drawn, -bound), bound).astype(held_as)


def setup_inputs(seed: int = 0) -> dict:
    seeds = jax.random.split(jax.random.key(seed), 7)
    return {
        "tokens": gaussian(seeds[0], (BATCH, SEQ_LEN, D), 1.0, 6.0, ((0, 8), (1, 32))),
        "qkv_base": draw_qkv_base(jax.random.fold_in(seeds[6], 71), 0),
        "qkv_dir": gaussian(seeds[2], (D, 3 * D), D ** -0.5, 0.1875, ((0, 8),)),
        "out_base": gaussian(seeds[3], (D, D), D ** -0.5, 0.1875, ((0, 8),)),
        "out_dir": gaussian(seeds[4], (D, D), D ** -0.5, 0.1875, ((0, 8),)),
        "alpha_index": jax.random.randint(seeds[5], (1,), 0, NALPHA).astype(jnp.int32),
    }


def normalize(tokens):
    widened = tokens.astype(jnp.float32)
    mean_square = lax.optimization_barrier(jnp.mean(widened * widened, axis=-1, keepdims=True))
    return (widened * lax.rsqrt(mean_square + 1e-06)).astype(jnp.bfloat16)

def masked_softmax(scores, allowed):
    masked = jnp.where(allowed, scores, -jnp.inf)
    row_peak = lax.optimization_barrier(jnp.max(masked, axis=-1, keepdims=True))
    weights = jnp.where(allowed, jnp.exp(masked - row_peak), 0.0)
    return (weights / lax.optimization_barrier(jnp.sum(weights, axis=-1, keepdims=True))).astype(jnp.bfloat16)

def rebuild(base_part, direction, step_alpha):
    return (base_part.astype(jnp.float32) + step_alpha * direction.astype(jnp.float32)).astype(jnp.bfloat16)

def reference(tokens, qkv_base, qkv_dir, out_base, out_dir, alpha_index):
    step_alpha = (alpha_index[0].astype(jnp.float32) + NALPHA) / (2.0 * NALPHA)
    w_qkv = rebuild(qkv_base, qkv_dir, step_alpha)
    w_out = rebuild(out_base, out_dir, step_alpha)
    head_dim = D // HEADS
    half_heads = HEADS // 2
    row_width = half_heads * head_dim
    row_count = SEQ_LEN // STRIDE
    score_scale = 1.0 / math.sqrt(head_dim)
    positions = jnp.arange(STRIDE)
    row_allowed = positions[None, :] <= positions[:, None]
    row_order = jnp.arange(row_count)
    col_allowed = row_order[None, :] <= row_order[:, None]

    def row_attend(row_block):
        widened = row_block.astype(jnp.float32)
        scores = jnp.einsum('qhd,khd->hqk', widened[:, 0], widened[:, 1]) * score_scale
        probabilities = masked_softmax(scores, row_allowed[None])
        return jnp.einsum('hqk,khd->qhd', probabilities.astype(jnp.float32), widened[:, 2]).astype(jnp.bfloat16)

    def one_sequence(sequence):
        normed = normalize(sequence)
        projected = jnp.dot(normed, w_qkv, preferred_element_type=jnp.float32).astype(jnp.bfloat16)
        split_heads = projected.reshape(row_count, STRIDE, 3, HEADS, head_dim)
        row_part = split_heads[:, :, :, :half_heads]
        col_part = split_heads[:, :, :, half_heads:].astype(jnp.float32)
        row_out = lax.map(row_attend, row_part)
        col_scores = jnp.einsum('rchd,schd->chrs', col_part[:, :, 0], col_part[:, :, 1]) * score_scale
        col_probs = masked_softmax(col_scores, col_allowed[None, None])
        col_out = jnp.einsum('chrs,schd->rchd', col_probs.astype(jnp.float32), col_part[:, :, 2]).astype(jnp.bfloat16)
        joined = jnp.concatenate([row_out.reshape(SEQ_LEN, row_width), col_out.reshape(SEQ_LEN, row_width)], 1)
        return jnp.dot(joined, w_out, preferred_element_type=jnp.float32).astype(jnp.bfloat16)
    return lax.map(one_sequence, tokens)
```

```python
import functools
import math

import jax
import jax.numpy as jnp
from jax import lax
from jax.experimental import pallas as pl
from jax.experimental.pallas import tpu as pltpu
from jax.sharding import PartitionSpec as P

D = 1024
HEADS = 16
STRIDE = 1024
NALPHA = 1024
HEAD_DIM = D // HEADS
HALF = D // 2
PAIR = 2 * HEAD_DIM
COLS_AT, ROWS_AT, OUT_AT = 0, 768, 1536
SLAB = 2048
F32, BF16 = jnp.float32, jnp.bfloat16
LOG2_SCALE = math.log2(math.e) / math.sqrt(HEAD_DIM)
BOTH = ("seq", "fsdp")


def split_index(i):
    s, f = divmod(i, 8)
    return s // 16, (s // 2) % 8, s % 2, f // 4, f % 4


def pairs(move):
    out = []
    for i in range(256):
        yl, z, c, yh, x = move(*split_index(i))
        out.append((i, ((yl * 8 + z) * 2 + c) * 8 + yh * 4 + x))
    return out


X_UP = pairs(lambda yl, z, c, yh, x: (yl, z, c, yh, (x + 1) % 4))
X_DOWN = pairs(lambda yl, z, c, yh, x: (yl, z, c, yh, (x - 1) % 4))
Y_NEAR = pairs(lambda yl, z, c, yh, x: (1 - yl, z, c, 1 - yh, x))
CORE = pairs(lambda yl, z, c, yh, x: (yl, z, 1 - c, yh, x))


def send(value, where):
    return lax.ppermute(value, BOTH, where)


def normalized(rows):
    mean_square = jnp.mean(rows * rows, axis=-1, keepdims=True)
    return (rows * lax.rsqrt(mean_square + 1e-06)).astype(BF16)


def fetch_weights(slabs, first, width, dest, sems):
    core = lax.axis_index("seq") % 2
    mine = lax.axis_index("fsdp")
    copies = []
    for n, slab in enumerate(slabs):
        half = core if n < 2 else 1 - core
        y_hi = mine // 4 if n % 2 == 0 else 1 - mine // 4
        for k in range(4):
            feature = pl.multiple_of((y_hi * 4 + (mine % 4 - k + 4) % 4) * 128, 128)
            copy = pltpu.make_async_copy(
                slab.at[k, :, pl.ds(first, width)],
                dest.at[half, pl.ds(feature, 128), :],
                sems.at[n * 4 + k],
            )
            copy.start()
            copies.append(copy)
    return copies


def soft_average(queries, keys, values_ones, mask):
    scores = lax.dot_general(queries, keys, (((1,), (1,)), ((), ())), preferred_element_type=F32)
    if mask is not None:
        width = mask.shape[1]
        last = scores[:, -width:] + mask
        scores = last if width == scores.shape[1] else jnp.concatenate([scores[:, :-width], last], 1)
    peak = jnp.max(scores, axis=-1, keepdims=True)
    weights = jnp.exp2((scores - peak) * LOG2_SCALE).astype(BF16)
    both = jnp.dot(weights, values_ones, preferred_element_type=F32)
    return both[:, :PAIR] / both[:, PAIR:]


def pair_attend(q, k, v, mask):
    rows = q.shape[0]
    first = lax.broadcasted_iota(jnp.int32, (rows, PAIR), 1) < HEAD_DIM
    nothing = jnp.zeros_like(q)
    values_ones = jnp.concatenate([v, jnp.ones_like(v)], 1)
    even = soft_average(jnp.where(first, q, nothing), k, values_ones, mask)
    odd = soft_average(jnp.where(first, nothing, q), k, values_ones, mask)
    return jnp.where(first, even, odd).astype(BF16)


def row_kernel(x_ref, s0, s1, s2, s3, o_ref, w, qkv, mask_ref, sems):
    copies = fetch_weights((s0, s1, s2, s3), ROWS_AT, 768, w, sems)
    block = 256
    row = lax.broadcasted_iota(jnp.int32, (block, block), 0)
    col = lax.broadcasted_iota(jnp.int32, (block, block), 1)
    mask_ref[...] = jnp.where(col <= row, 0.0, -jnp.inf)
    for copy in copies:
        copy.wait()

    def project(i, _):
        at = pl.ds(pl.multiple_of(i * block, block), block)
        normed = normalized(x_ref[at, :].astype(F32))
        for half in range(2):
            made = jnp.dot(normed, w[half], preferred_element_type=F32).astype(BF16)
            for which in range(3):
                for p in range(2):
                    lane = which * 256 + p * PAIR
                    qkv[which, half * 2 + p, at, :] = made[:, lane : lane + PAIR]
        return 0

    lax.fori_loop(0, STRIDE // block, project, 0)

    for p in range(4):
        for i in range(STRIDE // block):
            upto = (i + 1) * block
            o_ref[i * block : upto, p * PAIR : (p + 1) * PAIR] = pair_attend(
                qkv[0, p, i * block : upto, :],
                qkv[1, p, :upto, :],
                qkv[2, p, :upto, :],
                mask_ref[...],
            )


def col_kernel(x_ref, s0, s1, s2, s3, o_ref, w, mask_ref, sems):
    copies = fetch_weights((s0, s1, s2, s3), COLS_AT, 768, w, sems)
    rows = x_ref.shape[0]
    size = rows * 8
    at = lax.broadcasted_iota(jnp.int32, (size, size), 0)
    to = lax.broadcasted_iota(jnp.int32, (size, size), 1)
    meets = jnp.logical_and(at % 8 == to % 8, to <= at)
    mask_ref[...] = jnp.where(meets, 0.0, -jnp.inf)
    for copy in copies:
        copy.wait()
    for wide in range(x_ref.shape[1] // 16):
        taken = x_ref[:, wide * 16 : (wide + 1) * 16, :].astype(F32)
        parts = []
        for part in range(2):
            normed = normalized(taken[:, part * 8 : (part + 1) * 8, :].reshape(size, D))
            done = []
            for half in range(2):
                made = jnp.dot(normed, w[half], preferred_element_type=F32).astype(BF16)
                for p in range(2):
                    q, k, v = (
                        made[:, which * 256 + p * PAIR : which * 256 + (p + 1) * PAIR]
                        for which in range(3)
                    )
                    done.append(pair_attend(q, k, v, mask_ref[...]))
            parts.append(jnp.concatenate(done, 1).astype(F32).reshape(rows, 8, HALF))
        o_ref[:, wide * 16 : (wide + 1) * 16, :] = jnp.concatenate(parts, 1).astype(BF16)


def out_kernel(row_ref, col_ref, s0, s1, s2, s3, o_ref, w, sems):
    @pl.when(pl.program_id(0) == 0)
    def _():
        for copy in fetch_weights((s0, s1, s2, s3), OUT_AT, 512, w, sems):
            copy.wait()

    for half in range(2):
        total = jnp.dot(row_ref[...], w[half, :HALF, :], preferred_element_type=F32)
        total += jnp.dot(col_ref[...], w[half, HALF:, :], preferred_element_type=F32)
        o_ref[:, half * 512 : (half + 1) * 512] = total.astype(BF16)


ANY = pl.BlockSpec(memory_space=pl.ANY)
WHOLE = pl.BlockSpec(memory_space=pltpu.VMEM)
LIMIT = 48 << 20


def row_heads(sequence, slabs):
    return pl.pallas_call(
        row_kernel,
        out_shape=jax.ShapeDtypeStruct((STRIDE, HALF), BF16),
        in_specs=[WHOLE] + [ANY] * 4,
        out_specs=WHOLE,
        scratch_shapes=[
            pltpu.VMEM((2, D, 768), BF16),
            pltpu.VMEM((3, 4, STRIDE, PAIR), BF16),
            pltpu.VMEM((256, 256), F32),
            pltpu.SemaphoreType.DMA((16,)),
        ],
        compiler_params=pltpu.CompilerParams(vmem_limit_bytes=LIMIT),
        cost_estimate=pl.CostEstimate(
            flops=6_000_000_000, bytes_accessed=6 << 20, transcendentals=5_000_000
        ),
        name="row_heads",
    )(sequence, *slabs)


def col_heads(columns, slabs):
    rows, cols = columns.shape[:2]
    return pl.pallas_call(
        col_kernel,
        out_shape=jax.ShapeDtypeStruct((rows, cols, HALF), BF16),
        in_specs=[WHOLE] + [ANY] * 4,
        out_specs=WHOLE,
        scratch_shapes=[
            pltpu.VMEM((2, D, 768), BF16),
            pltpu.VMEM((rows * 8, rows * 8), F32),
            pltpu.SemaphoreType.DMA((16,)),
        ],
        compiler_params=pltpu.CompilerParams(vmem_limit_bytes=LIMIT),
        cost_estimate=pl.CostEstimate(
            flops=4_000_000_000, bytes_accessed=6 << 20, transcendentals=2_000_000
        ),
        name="col_heads",
    )(columns, *slabs)


def project_out(row_out, col_out, slabs):
    block = 256
    return pl.pallas_call(
        out_kernel,
        out_shape=jax.ShapeDtypeStruct((STRIDE, D), BF16),
        grid=(STRIDE // block,),
        in_specs=[pl.BlockSpec((block, HALF), lambda i: (i, 0))] * 2 + [ANY] * 4,
        out_specs=pl.BlockSpec((block, D), lambda i: (i, 0)),
        scratch_shapes=[pltpu.VMEM((2, D, 512), BF16), pltpu.SemaphoreType.DMA((16,))],
        compiler_params=pltpu.CompilerParams(vmem_limit_bytes=LIMIT),
        cost_estimate=pl.CostEstimate(
            flops=2_000_000_000, bytes_accessed=6 << 20, transcendentals=0
        ),
        name="project_out",
    )(row_out, col_out, *slabs)


def rebuild(base_part, direction, step_alpha):
    return (base_part.astype(F32) + step_alpha * direction.astype(F32)).astype(BF16)


def core_half(qkv, out, core):
    picked = lax.dynamic_index_in_dim(qkv.reshape(-1, 3, 2, 2, 256), core, 3, keepdims=False)
    parts = [picked[:, which, kind] for kind in (1, 0) for which in range(3)]
    parts.append(lax.dynamic_slice_in_dim(out, core * 512, 512, 1))
    return jnp.concatenate(parts, 1)


def shards(tokens, qkv_base, qkv_dir, out_base, out_dir, alpha_index):
    step_alpha = (alpha_index[0].astype(F32) + NALPHA) / (2.0 * NALPHA)
    core = lax.axis_index("seq") % 2
    sequence = tokens[0]
    columns = lax.all_to_all(
        sequence.reshape(32, 32, D), "seq", split_axis=0, concat_axis=0, tiled=True
    )
    own = rebuild(
        core_half(qkv_base, out_base, core), core_half(qkv_dir, out_dir, core), step_alpha
    )

    def around(piece):
        below, above = send(piece, X_UP), send(piece, X_DOWN)
        far = jnp.concatenate(
            [send(below[:, : SLAB // 2], X_UP), send(above[:, SLAB // 2 :], X_DOWN)], 1
        )
        return jnp.stack([piece, below, far, above])

    other = send(own, Y_NEAR)
    near_slab = around(own)
    far_slab = around(other)
    slabs = (near_slab, far_slab, send(near_slab, CORE), send(far_slab, CORE))
    attended = col_heads(columns, slabs)
    col_out = lax.all_to_all(attended, "seq", split_axis=0, concat_axis=0, tiled=True)
    row_out = row_heads(sequence, slabs)
    return project_out(row_out, col_out.reshape(STRIDE, HALF), slabs)[None]


def solution(mesh):
    in_specs = (
        P("fsdp", "seq", None),
        P("fsdp", None),
        P("fsdp", None),
        P("fsdp", None),
        P("fsdp", None),
        P(),
    )
    out_specs = P("fsdp", "seq", None)
    return jax.shard_map(shards, mesh=mesh, in_specs=in_specs, out_specs=out_specs, check_vma=False)
```

```python
import math

import jax
import jax.numpy as jnp
from jax import lax
from jax.experimental import pallas as pl
from jax.experimental.pallas import tpu as pltpu
from jax.sharding import PartitionSpec as P

D = 1024
HEADS = 16
STRIDE = 1024
NALPHA = 1024
HEAD_DIM = D // HEADS
HALF = D // 2
PAIR = 2 * HEAD_DIM
COLS_AT, ROWS_AT, OUT_AT = 0, 768, 1536
SLAB = 2048
F32, BF16 = jnp.float32, jnp.bfloat16
LOG2_SCALE = math.log2(math.e) / math.sqrt(HEAD_DIM)
BOTH = ("seq", "fsdp")


def split_index(i):
    s, f = divmod(i, 8)
    return s // 16, (s // 2) % 8, s % 2, f // 4, f % 4


def pairs(move):
    out = []
    for i in range(256):
        yl, z, c, yh, x = move(*split_index(i))
        out.append((i, ((yl * 8 + z) * 2 + c) * 8 + yh * 4 + x))
    return out


X_UP = pairs(lambda yl, z, c, yh, x: (yl, z, c, yh, (x + 1) % 4))
X_DOWN = pairs(lambda yl, z, c, yh, x: (yl, z, c, yh, (x - 1) % 4))
Y_NEAR = pairs(lambda yl, z, c, yh, x: (1 - yl, z, c, 1 - yh, x))
CORE = pairs(lambda yl, z, c, yh, x: (yl, z, 1 - c, yh, x))


def send(value, where):
    return lax.ppermute(value, BOTH, where)


def normalized(rows):
    mean_square = jnp.mean(rows * rows, axis=-1, keepdims=True)
    return (rows * lax.rsqrt(mean_square + 1e-06)).astype(BF16)


def fetch_weights(slabs, first, width, dest, sems):
    core = lax.axis_index("seq") % 2
    mine = lax.axis_index("fsdp")
    copies = []
    for n, slab in enumerate(slabs):
        half = core if n < 2 else 1 - core
        y_hi = mine // 4 if n % 2 == 0 else 1 - mine // 4
        for k in range(4):
            feature = pl.multiple_of((y_hi * 4 + (mine % 4 - k + 4) % 4) * 128, 128)
            copy = pltpu.make_async_copy(
                slab.at[k, :, pl.ds(first, width)],
                dest.at[half, pl.ds(feature, 128), :],
                sems.at[n * 4 + k],
            )
            copy.start()
            copies.append(copy)
    return copies


def prep_kernel(alpha_ref, qb_ref, qd_ref, ob_ref, od_ref, o_ref):
    core = lax.axis_index("seq") % 2
    step_alpha = (alpha_ref[0].astype(F32) + NALPHA) / (2.0 * NALPHA)
    at = 0
    for kind in (1, 0):
        for which in range(3):
            lanes = pl.ds(pl.multiple_of(which * D + kind * HALF + core * 256, 256), 256)
            rebuilt = qb_ref[:, lanes].astype(F32) + step_alpha * qd_ref[:, lanes].astype(F32)
            o_ref[:, at : at + 256] = rebuilt.astype(BF16)
            at += 256
    lanes = pl.ds(pl.multiple_of(core * 512, 512), 512)
    rebuilt = ob_ref[:, lanes].astype(F32) + step_alpha * od_ref[:, lanes].astype(F32)
    o_ref[:, at:] = rebuilt.astype(BF16)


def soft_average(queries, keys, values_ones, mask):
    scores = lax.dot_general(queries, keys, (((1,), (1,)), ((), ())), preferred_element_type=F32)
    width = mask.shape[1]
    last = scores[:, -width:] + mask
    scores = last if width == scores.shape[1] else jnp.concatenate([scores[:, :-width], last], 1)
    peak = jnp.max(scores, axis=-1, keepdims=True)
    weights = jnp.exp2((scores - peak) * LOG2_SCALE).astype(BF16)
    both = jnp.dot(weights, values_ones, preferred_element_type=F32)
    return both[:, :PAIR] / both[:, PAIR:]


def lanes_of_first(rows):
    return lax.broadcasted_iota(jnp.int32, (rows, PAIR), 1) < HEAD_DIM


def pair_attend(q, k, v, mask):
    first = lanes_of_first(q.shape[0])
    nothing = jnp.zeros_like(q)
    values_ones = jnp.concatenate([v, jnp.ones_like(v)], 1)
    even = soft_average(jnp.where(first, q, nothing), k, values_ones, mask)
    odd = soft_average(jnp.where(first, nothing, q), k, values_ones, mask)
    return jnp.where(first, even, odd).astype(BF16)


def block_attend(q, k, v, mask):
    first = lanes_of_first(q.shape[0])
    nothing, one = jnp.zeros_like(q), jnp.ones_like(q)
    keys = jnp.concatenate([jnp.where(first, k, nothing), jnp.where(first, nothing, k)], 0)
    scores = lax.dot_general(q, keys, (((1,), (1,)), ((), ())), preferred_element_type=F32)
    weights = []
    for head in range(2):
        own = scores[:, head * 128 : (head + 1) * 128] + mask
        peak = jnp.max(own, axis=-1, keepdims=True)
        weights.append(jnp.exp2((own - peak) * LOG2_SCALE).astype(BF16))
    values = jnp.concatenate(
        [
            jnp.concatenate([jnp.where(first, v, nothing), jnp.where(first, one, nothing)], 1),
            jnp.concatenate([jnp.where(first, nothing, v), jnp.where(first, nothing, one)], 1),
        ],
        0,
    )
    both = jnp.dot(jnp.concatenate(weights, 1), values, preferred_element_type=F32)
    return (both[:, :PAIR] / both[:, PAIR:]).astype(BF16)


def row_kernel(x_ref, s0, s1, s2, s3, part_hbm, wc_hbm, w, wo, qkv, attended, mask_ref, part, sems, sems_o, sems_part):
    slabs = (s0, s1, s2, s3)
    copies = fetch_weights(slabs, ROWS_AT, 768, w, sems)
    copies_out = fetch_weights(slabs, OUT_AT, 512, wo, sems_o)
    block = 256
    row = lax.broadcasted_iota(jnp.int32, (block, block), 0)
    col = lax.broadcasted_iota(jnp.int32, (block, block), 1)
    mask_ref[...] = jnp.where(col <= row, 0.0, -jnp.inf)
    for copy in copies:
        copy.wait()

    def project(i, _):
        at = pl.ds(pl.multiple_of(i * block, block), block)
        normed = normalized(x_ref[at, :].astype(F32))
        for half in range(2):
            made = jnp.dot(normed, w[half], preferred_element_type=F32).astype(BF16)
            for which in range(3):
                for p in range(2):
                    lane = which * 256 + p * PAIR
                    qkv[which, half * 2 + p, at, :] = made[:, lane : lane + PAIR]
        return 0

    lax.fori_loop(0, STRIDE // block, project, 0)

    for p in range(4):
        for i in range(STRIDE // block):
            upto = (i + 1) * block
            attended[i * block : upto, p * PAIR : (p + 1) * PAIR] = pair_attend(
                qkv[0, p, i * block : upto, :],
                qkv[1, p, :upto, :],
                qkv[2, p, :upto, :],
                mask_ref[...],
            )
    for copy in copies_out:
        copy.wait()

    copies = [pltpu.make_async_copy(wo.at[:, pl.ds(HALF, HALF), :], wc_hbm, sems.at[0])]
    copies[0].start()
    for i in range(STRIDE // block):
        at = slice(i * block, (i + 1) * block)
        for half in range(2):
            part[at, half * 512 : (half + 1) * 512] = jnp.dot(
                attended[at, :], wo[half, :HALF, :], preferred_element_type=F32
            )
        copies.append(pltpu.make_async_copy(part.at[at, :], part_hbm.at[at, :], sems_part.at[i]))
        copies[-1].start()
    for copy in copies:
        copy.wait()


def sequence_row(place):
    z = place // 4
    z = (z % 2) * 4 + (z // 2 % 2) * 2 + z // 4
    return (place // 2 % 2) * 16 + z * 2 + place % 2


def col_kernel(x_hbm, s0, s1, s2, s3, o_hbm, x, w, out, mask_ref, sort_ref, sems, sems_x, sems_o):
    wide = 16
    steps = x.shape[1] // wide
    arrive, leave = [], []
    for i in range(steps):
        at = pl.ds(i * wide, wide)
        arrive.append(pltpu.make_async_copy(x_hbm.at[:, at, :], x.at[:, at, :], sems_x.at[i]))
        leave.append(pltpu.make_async_copy(out.at[:, at, :], o_hbm.at[:, at, :], sems_o.at[i]))
    arrive[0].start()
    weights = fetch_weights((s0, s1, s2, s3), COLS_AT, 768, w, sems)
    for copy in arrive[1:]:
        copy.start()
    size = 256
    at = lax.broadcasted_iota(jnp.int32, (128, 128), 0)
    to = lax.broadcasted_iota(jnp.int32, (128, 128), 1)
    meets = jnp.logical_and(at // 32 == to // 32, to <= at)
    mask_ref[...] = jnp.where(meets, 0.0, -jnp.inf)
    new = lax.broadcasted_iota(jnp.int32, (size, size), 0)
    old = lax.broadcasted_iota(jnp.int32, (size, size), 1)
    moves = jnp.logical_and(new // 32 == old % 8, new % 32 == sequence_row(old // 8))
    sort_ref[...] = jnp.where(moves, 1.0, 0.0).astype(BF16)

    for i in range(steps):
        arrive[i].wait()
        taken = x[:, i * wide : (i + 1) * wide, :].astype(F32)
        sorted_parts = []
        for part in range(2):
            normed = normalized(taken[:, part * 8 : (part + 1) * 8, :].reshape(size, D))
            sorted_parts.append(
                jnp.dot(sort_ref[...], normed, preferred_element_type=F32).astype(BF16)
            )
        if i == 0:
            for copy in weights:
                copy.wait()
        backs = []
        for normed in sorted_parts:
            done = []
            for half in range(2):
                made = jnp.dot(normed, w[half], preferred_element_type=F32).astype(BF16)
                for p in range(2):
                    q, k, v = (
                        made[:, which * 256 + p * PAIR : which * 256 + (p + 1) * PAIR]
                        for which in range(3)
                    )
                    blocks = [
                        block_attend(q[n : n + 128], k[n : n + 128], v[n : n + 128], mask_ref[...])
                        for n in (0, 128)
                    ]
                    done.append(jnp.concatenate(blocks, 0))
            back = lax.dot_general(
                sort_ref[...],
                jnp.concatenate(done, 1),
                (((0,), (0,)), ((), ())),
                preferred_element_type=F32,
            )
            backs.append(back.reshape(32, 8, HALF))
        out[:, i * wide : (i + 1) * wide, :] = jnp.concatenate(backs, 1).astype(BF16)
        leave[i].start()
    for copy in leave:
        copy.wait()


def out_kernel(part_hbm, col_hbm, w_hbm, o_hbm, part, col, w, out, sem_w, sems_p, sems_c, sems_o):
    block = 256
    weights = pltpu.make_async_copy(w_hbm, w, sem_w.at[0])
    weights.start()
    parts, cols, outs = [], [], []
    for i in range(STRIDE // block):
        at = pl.ds(i * block, block)
        parts.append(pltpu.make_async_copy(part_hbm.at[at, :], part.at[at, :], sems_p.at[i]))
        cols.append(pltpu.make_async_copy(col_hbm.at[at, :], col.at[at, :], sems_c.at[i]))
        outs.append(pltpu.make_async_copy(out.at[at, :], o_hbm.at[at, :], sems_o.at[i]))
        cols[i].start()
        parts[i].start()
    weights.wait()
    for i in range(STRIDE // block):
        at = slice(i * block, (i + 1) * block)
        cols[i].wait()
        parts[i].wait()
        for half in range(2):
            lanes = slice(half * 512, (half + 1) * 512)
            total = part[at, lanes] + jnp.dot(
                col[at, :], w[half], preferred_element_type=F32
            )
            out[at, lanes] = total.astype(BF16)
        outs[i].start()
    for copy in outs:
        copy.wait()


ANY = pl.BlockSpec(memory_space=pl.ANY)
WHOLE = pl.BlockSpec(memory_space=pltpu.VMEM)
FAR = pl.BlockSpec(memory_space=pltpu.HBM)
DMA = pltpu.SemaphoreType.DMA


def limit(mib):
    return pltpu.CompilerParams(vmem_limit_bytes=mib << 20)


def rebuilt_half(alpha_index, *parts):
    return pl.pallas_call(
        prep_kernel,
        out_shape=jax.ShapeDtypeStruct((parts[0].shape[0], SLAB), BF16),
        in_specs=[pl.BlockSpec(memory_space=pltpu.SMEM)] + [WHOLE] * 4,
        out_specs=WHOLE,
        compiler_params=limit(16),
        name="rebuilt_half",
    )(alpha_index, *parts)


def row_heads(sequence, slabs):
    return pl.pallas_call(
        row_kernel,
        out_shape=(
            jax.ShapeDtypeStruct((STRIDE, D), F32),
            jax.ShapeDtypeStruct((2, HALF, 512), BF16),
        ),
        in_specs=[WHOLE] + [ANY] * 4,
        out_specs=(FAR, FAR),
        scratch_shapes=[
            pltpu.VMEM((2, D, 768), BF16),
            pltpu.VMEM((2, D, 512), BF16),
            pltpu.VMEM((3, 4, STRIDE, PAIR), BF16),
            pltpu.VMEM((STRIDE, HALF), BF16),
            pltpu.VMEM((256, 256), F32),
            pltpu.VMEM((STRIDE, D), F32),
            DMA((16,)),
            DMA((16,)),
            DMA((4,)),
        ],
        compiler_params=limit(63),
        cost_estimate=pl.CostEstimate(
            flops=7_000_000_000, bytes_accessed=12 << 20, transcendentals=5_000_000
        ),
        name="row_heads",
    )(sequence, *slabs)


def col_heads(columns, slabs):
    rows, cols = columns.shape[:2]
    return pl.pallas_call(
        col_kernel,
        out_shape=jax.ShapeDtypeStruct((rows, cols, HALF), BF16),
        in_specs=[FAR] + [ANY] * 4,
        out_specs=FAR,
        scratch_shapes=[
            pltpu.VMEM((rows, cols, D), BF16),
            pltpu.VMEM((2, D, 768), BF16),
            pltpu.VMEM((rows, cols, HALF), BF16),
            pltpu.VMEM((128, 128), F32),
            pltpu.VMEM((256, 256), BF16),
            DMA((16,)),
            DMA((cols // 16,)),
            DMA((cols // 16,)),
        ],
        compiler_params=limit(63),
        cost_estimate=pl.CostEstimate(
            flops=4_000_000_000, bytes_accessed=6 << 20, transcendentals=1_000_000
        ),
        name="col_heads",
    )(columns, *slabs)


def project_out(row_part, col_out, weights):
    return pl.pallas_call(
        out_kernel,
        out_shape=jax.ShapeDtypeStruct((STRIDE, D), BF16),
        in_specs=[FAR] * 3,
        out_specs=FAR,
        scratch_shapes=[
            pltpu.VMEM((STRIDE, D), F32),
            pltpu.VMEM((STRIDE, HALF), BF16),
            pltpu.VMEM((2, HALF, 512), BF16),
            pltpu.VMEM((STRIDE, D), BF16),
            DMA((1,)),
            DMA((4,)),
            DMA((4,)),
            DMA((4,)),
        ],
        compiler_params=limit(63),
        cost_estimate=pl.CostEstimate(
            flops=1_000_000_000, bytes_accessed=8 << 20, transcendentals=0
        ),
        name="project_out",
    )(row_part, col_out, weights)


ORDER = [sequence_row(place) for place in range(32)]


def exchange(blocks):
    return lax.all_to_all(
        blocks, "seq", split_axis=0, concat_axis=0, tiled=True, axis_index_groups=[ORDER]
    )


def shards(tokens, qkv_base, qkv_dir, out_base, out_dir, alpha_index):
    sequence = tokens[0]
    columns = exchange(sequence.reshape(32, 32, D))
    own = rebuilt_half(alpha_index, qkv_base, qkv_dir, out_base, out_dir)

    def around(piece):
        below, above = send(piece, X_UP), send(piece, X_DOWN)
        far = jnp.concatenate(
            [send(below[:, : SLAB // 2], X_UP), send(above[:, SLAB // 2 :], X_DOWN)], 1
        )
        return jnp.stack([piece, below, far, above])

    other = send(own, Y_NEAR)
    near_slab = around(own)
    far_slab = around(other)
    slabs = (near_slab, far_slab, send(near_slab, CORE), send(far_slab, CORE))
    attended = col_heads(columns, slabs)
    col_out = exchange(attended)
    row_part, weights = row_heads(sequence, slabs)
    return project_out(row_part, col_out.reshape(STRIDE, HALF), weights)[None]


def solution(mesh):
    in_specs = (
        P("fsdp", "seq", None),
        P("fsdp", None),
        P("fsdp", None),
        P("fsdp", None),
        P("fsdp", None),
        P(),
    )
    out_specs = P("fsdp", "seq", None)
    return jax.shard_map(shards, mesh=mesh, in_specs=in_specs, out_specs=out_specs, check_vma=False)
```

```python
import math

import jax
import jax.numpy as jnp
from jax import lax
from jax.experimental import pallas as pl
from jax.experimental.pallas import tpu as pltpu
from jax.sharding import PartitionSpec as P

D = 1024
HEADS = 16
STRIDE = 1024
NALPHA = 1024
HEAD_DIM = D // HEADS
HALF = D // 2
PAIR = 2 * HEAD_DIM
COLS, REST = 768, 1280
F32, BF16 = jnp.float32, jnp.bfloat16
LOG2_SCALE = math.log2(math.e) / math.sqrt(HEAD_DIM)
BOTH = ("seq", "fsdp")


def split_index(i):
    s, f = divmod(i, 8)
    return s // 16, (s // 2) % 8, s % 2, f // 4, f % 4


def pairs(move):
    out = []
    for i in range(256):
        yl, z, c, yh, x = move(*split_index(i))
        out.append((i, ((yl * 8 + z) * 2 + c) * 8 + yh * 4 + x))
    return out


def hop(other_y, dx):
    return pairs(
        lambda yl, z, c, yh, x: (yl ^ other_y, z, c, yh ^ other_y, (x + dx) % 4)
    )


HOPS = [hop(other_y, dx) for other_y in range(2) for dx in range(4)]
CORE = pairs(lambda yl, z, c, yh, x: (yl, z, 1 - c, yh, x))


def send(value, where):
    return lax.ppermute(value, BOTH, where)


def normalized(rows):
    mean_square = jnp.mean(rows * rows, axis=-1, keepdims=True)
    return (rows * lax.rsqrt(mean_square + 1e-06)).astype(BF16)


def fetch_weights(slabs, first, width, dest, sems):
    core = lax.axis_index("seq") % 2
    mine = lax.axis_index("fsdp")
    copies = []
    for n, slab in enumerate(slabs):
        half = core if n == 0 else 1 - core
        for k in range(8):
            y_hi = mine // 4 if k % 2 == 0 else 1 - mine // 4
            feature = pl.multiple_of((y_hi * 4 + (mine % 4 - k // 2 + 4) % 4) * 128, 128)
            copy = pltpu.make_async_copy(
                slab.at[k, :, pl.ds(first, width)],
                dest.at[half, pl.ds(feature, 128), :],
                sems.at[n * 8 + k],
            )
            copy.start()
            copies.append(copy)
    return copies


def prep_kernel(alpha_ref, qb_ref, qd_ref, ob_ref, od_ref, cols_ref, rest_ref):
    core = lax.axis_index("seq") % 2
    step_alpha = (alpha_ref[0].astype(F32) + NALPHA) / (2.0 * NALPHA)
    for kind, to_ref in ((1, cols_ref), (0, rest_ref)):
        for which in range(3):
            lanes = pl.ds(pl.multiple_of(which * D + kind * HALF + core * 256, 256), 256)
            rebuilt = qb_ref[:, lanes].astype(F32) + step_alpha * qd_ref[:, lanes].astype(F32)
            to_ref[:, which * 256 : (which + 1) * 256] = rebuilt.astype(BF16)
    lanes = pl.ds(pl.multiple_of(core * 512, 512), 512)
    rebuilt = ob_ref[:, lanes].astype(F32) + step_alpha * od_ref[:, lanes].astype(F32)
    rest_ref[:, 768:] = rebuilt.astype(BF16)


def soft_average(queries, keys, values_ones, mask):
    scores = lax.dot_general(queries, keys, (((1,), (1,)), ((), ())), preferred_element_type=F32)
    width = mask.shape[1]
    last = scores[:, -width:] + mask
    scores = last if width == scores.shape[1] else jnp.concatenate([scores[:, :-width], last], 1)
    peak = jnp.max(scores, axis=-1, keepdims=True)
    weights = jnp.exp2((scores - peak) * LOG2_SCALE).astype(BF16)
    both = jnp.dot(weights, values_ones, preferred_element_type=F32)
    return both[:, :PAIR] / both[:, PAIR:]


def lanes_of_first(rows):
    return lax.broadcasted_iota(jnp.int32, (rows, PAIR), 1) < HEAD_DIM


def pair_attend(q, k, v, mask):
    first = lanes_of_first(q.shape[0])
    nothing = jnp.zeros_like(q)
    values_ones = jnp.concatenate([v, jnp.ones_like(v)], 1)
    even = soft_average(jnp.where(first, q, nothing), k, values_ones, mask)
    odd = soft_average(jnp.where(first, nothing, q), k, values_ones, mask)
    return jnp.where(first, even, odd).astype(BF16)


def block_scores(q, k):
    first = lanes_of_first(q.shape[0])
    nothing = jnp.zeros_like(q)
    keys = jnp.concatenate([jnp.where(first, k, nothing), jnp.where(first, nothing, k)], 0)
    return lax.dot_general(q, keys, (((1,), (1,)), ((), ())), preferred_element_type=F32)


def block_weights(scores, mask):
    weights = []
    for head in range(2):
        own = scores[:, head * 128 : (head + 1) * 128] + mask
        peak = jnp.max(own, axis=-1, keepdims=True)
        weights.append(jnp.exp2((own - peak) * LOG2_SCALE).astype(BF16))
    return jnp.concatenate(weights, 1)


def block_average(weights, v):
    first = lanes_of_first(v.shape[0])
    nothing, one = jnp.zeros_like(v), jnp.ones_like(v)
    values = jnp.concatenate(
        [
            jnp.concatenate([jnp.where(first, v, nothing), jnp.where(first, one, nothing)], 1),
            jnp.concatenate([jnp.where(first, nothing, v), jnp.where(first, nothing, one)], 1),
        ],
        0,
    )
    both = jnp.dot(weights, values, preferred_element_type=F32)
    return (both[:, :PAIR] / both[:, PAIR:]).astype(BF16)


def row_kernel(x_ref, s0, s1, part_hbm, wc_hbm, w, wo, qkv, attended, mask_ref, part, sems, sems_o, sems_part):
    slabs = (s0, s1)
    copies = fetch_weights(slabs, 0, 768, w, sems)
    copies_out = fetch_weights(slabs, 768, 512, wo, sems_o)
    block = 256
    row = lax.broadcasted_iota(jnp.int32, (block, block), 0)
    col = lax.broadcasted_iota(jnp.int32, (block, block), 1)
    mask_ref[...] = jnp.where(col <= row, 0.0, -jnp.inf)
    for copy in copies:
        copy.wait()

    def project(i, _):
        at = pl.ds(pl.multiple_of(i * block, block), block)
        normed = normalized(x_ref[at, :].astype(F32))
        for half in range(2):
            made = jnp.dot(normed, w[half], preferred_element_type=F32).astype(BF16)
            for which in range(3):
                for p in range(2):
                    lane = which * 256 + p * PAIR
                    qkv[which, half * 2 + p, at, :] = made[:, lane : lane + PAIR]
        return 0

    lax.fori_loop(0, STRIDE // block, project, 0)

    for p in range(4):
        for i in range(STRIDE // block):
            upto = (i + 1) * block
            attended[i * block : upto, p * PAIR : (p + 1) * PAIR] = pair_attend(
                qkv[0, p, i * block : upto, :],
                qkv[1, p, :upto, :],
                qkv[2, p, :upto, :],
                mask_ref[...],
            )
    for copy in copies_out:
        copy.wait()

    copies = [pltpu.make_async_copy(wo.at[:, pl.ds(HALF, HALF), :], wc_hbm, sems.at[0])]
    copies[0].start()
    for i in range(STRIDE // block):
        at = slice(i * block, (i + 1) * block)
        for half in range(2):
            part[at, half * 512 : (half + 1) * 512] = jnp.dot(
                attended[at, :], wo[half, :HALF, :], preferred_element_type=F32
            )
        copies.append(pltpu.make_async_copy(part.at[at, :], part_hbm.at[at, :], sems_part.at[i]))
        copies[-1].start()
    for copy in copies:
        copy.wait()


def sequence_row(place):
    z = ((place >> 2) & 1) * 4 + ((place >> 3) & 1) * 2 + (place >> 4)
    return ((place >> 1) & 1) * 16 + z * 2 + (place & 1)


def place_of(row):
    z = ((row >> 1) & 1) * 4 + ((row >> 2) & 1) * 2 + ((row >> 3) & 1)
    return z * 4 + (row >> 4) * 2 + (row & 1)


WIDE = 16
STEP = 32 * WIDE


def one_hot(ref, lane_of):
    wanted = lane_of(lax.broadcasted_iota(jnp.int32, (STEP, 128), 0))
    lane = lax.broadcasted_iota(jnp.int32, (STEP, 128), 1)
    for at in range(0, STEP, 128):
        ref[:, at : at + 128] = jnp.where(wanted == lane + at, 1.0, 0.0).astype(BF16)


def col_kernel(
    x_hbm, s0, s1, o_hbm, x, w, out, mask_ref, sort_ref, back_ref, normed_ref, sems, sems_x, sems_o
):
    steps = x.shape[1] // WIDE
    arrive, leave = [], []
    for i in range(steps):
        at = pl.ds(i * WIDE, WIDE)
        arrive.append(pltpu.make_async_copy(x_hbm.at[:, at, :], x.at[:, at, :], sems_x.at[i]))
        leave.append(pltpu.make_async_copy(out.at[:, at, :], o_hbm.at[:, at, :], sems_o.at[i]))
        arrive[i].start()
    weights = fetch_weights((s0, s1), 0, 768, w, sems)
    at = lax.broadcasted_iota(jnp.int32, (128, 128), 0)
    to = lax.broadcasted_iota(jnp.int32, (128, 128), 1)
    meets = jnp.logical_and(at // 32 == to // 32, to <= at)
    mask_ref[...] = jnp.where(meets, 0.0, -jnp.inf)
    one_hot(sort_ref, lambda new: place_of(new & 31) * WIDE + (new >> 5))
    one_hot(back_ref, lambda old: (old & (WIDE - 1)) * 32 + sequence_row(old >> 4))
    for i in range(steps):
        arrive[i].wait()
        taken = x[:, i * WIDE : (i + 1) * WIDE, :].reshape(STEP, D)
        for half in range(2):
            rows = slice(half * 256, half * 256 + 256)
            ordered = jnp.dot(sort_ref[rows, :], taken, preferred_element_type=F32)
            normed_ref[i * STEP + half * 256 : i * STEP + half * 256 + 256, :] = normalized(ordered)
    for copy in weights:
        copy.wait()
    for i in range(steps):
        attended = []
        for group in range(STEP // 256):
            start = i * STEP + group * 256
            parts = [
                jnp.dot(
                    normed_ref[start : start + 256, :], w[half], preferred_element_type=F32
                ).astype(BF16)
                for half in range(2)
            ]
            blocks = []
            for made in parts:
                for p in range(2):
                    for n in (0, 128):
                        blocks.append(
                            [
                                made[n : n + 128, which * 256 + p * PAIR : which * 256 + (p + 1) * PAIR]
                                for which in range(3)
                            ]
                        )
            scores = [block_scores(q, k) for q, k, _ in blocks]
            shares = [block_weights(score, mask_ref[...]) for score in scores]
            done = [block_average(share, v) for share, (_, _, v) in zip(shares, blocks)]
            attended.append(jnp.concatenate(
                [jnp.concatenate(done[n::2], 1) for n in range(2)], 0
            ))
        back = jnp.dot(
            back_ref[...], jnp.concatenate(attended, 0), preferred_element_type=F32
        ).astype(BF16)
        out[:, i * WIDE : (i + 1) * WIDE, :] = back.reshape(32, WIDE, HALF)
        leave[i].start()
    for copy in leave:
        copy.wait()


def out_kernel(part_hbm, col_hbm, w_hbm, o_hbm, part, col, w, out, sem_w, sems_p, sems_c, sems_o):
    block = 256
    weights = pltpu.make_async_copy(w_hbm, w, sem_w.at[0])
    weights.start()
    parts, cols, outs = [], [], []
    for i in range(STRIDE // block):
        at = pl.ds(i * block, block)
        parts.append(pltpu.make_async_copy(part_hbm.at[at, :], part.at[at, :], sems_p.at[i]))
        cols.append(pltpu.make_async_copy(col_hbm.at[at, :], col.at[at, :], sems_c.at[i]))
        outs.append(pltpu.make_async_copy(out.at[at, :], o_hbm.at[at, :], sems_o.at[i]))
        cols[i].start()
        parts[i].start()
    weights.wait()
    for i in range(STRIDE // block):
        at = slice(i * block, (i + 1) * block)
        cols[i].wait()
        parts[i].wait()
        for half in range(2):
            lanes = slice(half * 512, (half + 1) * 512)
            total = part[at, lanes] + jnp.dot(
                col[at, :], w[half], preferred_element_type=F32
            )
            out[at, lanes] = total.astype(BF16)
        outs[i].start()
    for copy in outs:
        copy.wait()


ANY = pl.BlockSpec(memory_space=pl.ANY)
WHOLE = pl.BlockSpec(memory_space=pltpu.VMEM)
FAR = pl.BlockSpec(memory_space=pltpu.HBM)
DMA = pltpu.SemaphoreType.DMA


def limit(mib):
    return pltpu.CompilerParams(vmem_limit_bytes=mib << 20)


def rebuilt_half(alpha_index, *parts):
    return pl.pallas_call(
        prep_kernel,
        out_shape=[
            jax.ShapeDtypeStruct((parts[0].shape[0], width), BF16) for width in (COLS, REST)
        ],
        in_specs=[pl.BlockSpec(memory_space=pltpu.SMEM)] + [WHOLE] * 4,
        out_specs=[WHOLE] * 2,
        compiler_params=limit(16),
        name="rebuilt_half",
    )(alpha_index, *parts)


def row_heads(sequence, slabs):
    return pl.pallas_call(
        row_kernel,
        out_shape=(
            jax.ShapeDtypeStruct((STRIDE, D), F32),
            jax.ShapeDtypeStruct((2, HALF, 512), BF16),
        ),
        in_specs=[WHOLE] + [ANY] * 2,
        out_specs=(FAR, FAR),
        scratch_shapes=[
            pltpu.VMEM((2, D, 768), BF16),
            pltpu.VMEM((2, D, 512), BF16),
            pltpu.VMEM((3, 4, STRIDE, PAIR), BF16),
            pltpu.VMEM((STRIDE, HALF), BF16),
            pltpu.VMEM((256, 256), F32),
            pltpu.VMEM((STRIDE, D), F32),
            DMA((16,)),
            DMA((16,)),
            DMA((4,)),
        ],
        compiler_params=limit(63),
        cost_estimate=pl.CostEstimate(
            flops=7_000_000_000, bytes_accessed=12 << 20, transcendentals=5_000_000
        ),
        name="row_heads",
    )(sequence, *slabs)


def col_heads(columns, slabs):
    rows, cols = columns.shape[:2]
    return pl.pallas_call(
        col_kernel,
        out_shape=jax.ShapeDtypeStruct((rows, cols, HALF), BF16),
        in_specs=[FAR] + [ANY] * 2,
        out_specs=FAR,
        scratch_shapes=[
            pltpu.VMEM((rows, cols, D), BF16),
            pltpu.VMEM((2, D, 768), BF16),
            pltpu.VMEM((rows, cols, HALF), BF16),
            pltpu.VMEM((128, 128), F32),
            pltpu.VMEM((STEP, STEP), BF16),
            pltpu.VMEM((STEP, STEP), BF16),
            pltpu.VMEM((rows * cols, D), BF16),
            DMA((16,)),
            DMA((cols // WIDE,)),
            DMA((cols // WIDE,)),
        ],
        compiler_params=limit(63),
        cost_estimate=pl.CostEstimate(
            flops=4_000_000_000, bytes_accessed=6 << 20, transcendentals=1_000_000
        ),
        name="col_heads",
    )(columns, *slabs)


def project_out(row_part, col_out, weights):
    return pl.pallas_call(
        out_kernel,
        out_shape=jax.ShapeDtypeStruct((STRIDE, D), BF16),
        in_specs=[FAR] * 3,
        out_specs=FAR,
        scratch_shapes=[
            pltpu.VMEM((STRIDE, D), F32),
            pltpu.VMEM((STRIDE, HALF), BF16),
            pltpu.VMEM((2, HALF, 512), BF16),
            pltpu.VMEM((STRIDE, D), BF16),
            DMA((1,)),
            DMA((4,)),
            DMA((4,)),
            DMA((4,)),
        ],
        compiler_params=limit(63),
        cost_estimate=pl.CostEstimate(
            flops=1_000_000_000, bytes_accessed=8 << 20, transcendentals=0
        ),
        name="project_out",
    )(row_part, col_out, weights)


ORDER = [sequence_row(place) for place in range(32)]


def exchange(blocks):
    return lax.all_to_all(
        blocks, "seq", split_axis=0, concat_axis=0, tiled=True, axis_index_groups=[ORDER]
    )


def gathered(own):
    both = jnp.stack([own, send(own, HOPS[4])])
    slab = jnp.concatenate([both] + [send(both, where) for where in HOPS[1:4]])
    return slab, send(slab, CORE)


def shards(tokens, qkv_base, qkv_dir, out_base, out_dir, alpha_index):
    sequence = tokens[0]
    columns = exchange(sequence.reshape(32, 32, D))
    own_cols, own_rest = rebuilt_half(alpha_index, qkv_base, qkv_dir, out_base, out_dir)
    col_slabs = gathered(own_cols)
    rest_slabs = gathered(own_rest)
    attended = col_heads(columns, col_slabs)
    col_out = exchange(attended)
    row_part, weights = row_heads(sequence, rest_slabs)
    return project_out(row_part, col_out.reshape(STRIDE, HALF), weights)[None]


def solution(mesh):
    in_specs = (
        P("fsdp", "seq", None),
        P("fsdp", None),
        P("fsdp", None),
        P("fsdp", None),
        P("fsdp", None),
        P(),
    )
    out_specs = P("fsdp", "seq", None)
    return jax.shard_map(shards, mesh=mesh, in_specs=in_specs, out_specs=out_specs, check_vma=False)
```

```python
import math

import jax
import jax.numpy as jnp
from jax import lax
from jax.experimental import pallas as pl
from jax.experimental.pallas import tpu as pltpu
from jax.sharding import PartitionSpec as P

D = 1024
HEADS = 16
STRIDE = 1024
NALPHA = 1024
HEAD_DIM = D // HEADS
HALF = D // 2
PAIR = 2 * HEAD_DIM
COLS, REST = 768, 1280
F32, BF16 = jnp.float32, jnp.bfloat16
LOG2_SCALE = math.log2(math.e) / math.sqrt(HEAD_DIM)
BOTH = ("seq", "fsdp")


def split_index(i):
    s, f = divmod(i, 8)
    return s // 16, (s // 2) % 8, s % 2, f // 4, f % 4


def pairs(move):
    out = []
    for i in range(256):
        yl, z, c, yh, x = move(*split_index(i))
        out.append((i, ((yl * 8 + z) * 2 + c) * 8 + yh * 4 + x))
    return out


def hop(other_y, dx):
    return pairs(
        lambda yl, z, c, yh, x: (yl ^ other_y, z, c, yh ^ other_y, (x + dx) % 4)
    )


CORE = pairs(lambda yl, z, c, yh, x: (yl, z, 1 - c, yh, x))


def send(value, where):
    return lax.ppermute(value, BOTH, where)


def normalized(rows):
    mean_square = jnp.mean(rows * rows, axis=-1, keepdims=True)
    return (rows * lax.rsqrt(mean_square + 1e-06)).astype(BF16)


def fetch_weights(slabs, first, width, dest, sems):
    core = lax.axis_index("seq") % 2
    mine = lax.axis_index("fsdp")
    copies = []
    for n, slab in enumerate(slabs):
        half = core if n < 4 else 1 - core
        for k in range(2):
            y_hi = mine // 4 if k == 0 else 1 - mine // 4
            feature = pl.multiple_of((y_hi * 4 + (mine % 4 - n % 4 + 4) % 4) * 128, 128)
            copy = pltpu.make_async_copy(
                slab.at[k, :, pl.ds(first, width)],
                dest.at[half, pl.ds(feature, 128), :],
                sems.at[n * 2 + k],
            )
            copy.start()
            copies.append(copy)
    return copies


def prep_kernel(alpha_ref, qb_ref, qd_ref, ob_ref, od_ref, cols_ref, rest_ref):
    core = lax.axis_index("seq") % 2
    step_alpha = (alpha_ref[0].astype(F32) + NALPHA) / (2.0 * NALPHA)
    for kind, to_ref in ((1, cols_ref), (0, rest_ref)):
        for which in range(3):
            lanes = pl.ds(pl.multiple_of(which * D + kind * HALF + core * 256, 256), 256)
            rebuilt = qb_ref[:, lanes].astype(F32) + step_alpha * qd_ref[:, lanes].astype(F32)
            to_ref[:, which * 256 : (which + 1) * 256] = rebuilt.astype(BF16)
    lanes = pl.ds(pl.multiple_of(core * 512, 512), 512)
    rebuilt = ob_ref[:, lanes].astype(F32) + step_alpha * od_ref[:, lanes].astype(F32)
    rest_ref[:, 768:] = rebuilt.astype(BF16)


def soft_average(queries, keys, values_ones, mask):
    scores = lax.dot_general(queries, keys, (((1,), (1,)), ((), ())), preferred_element_type=F32)
    width = mask.shape[1]
    last = scores[:, -width:] + mask
    scores = last if width == scores.shape[1] else jnp.concatenate([scores[:, :-width], last], 1)
    peak = jnp.max(scores, axis=-1, keepdims=True)
    weights = jnp.exp2((scores - peak) * LOG2_SCALE).astype(BF16)
    both = jnp.dot(weights, values_ones, preferred_element_type=F32)
    return both[:, :PAIR] / both[:, PAIR:]


def lanes_of_first(rows):
    return lax.broadcasted_iota(jnp.int32, (rows, PAIR), 1) < HEAD_DIM


def pair_attend(q, k, v, mask):
    first = lanes_of_first(q.shape[0])
    nothing = jnp.zeros_like(q)
    values_ones = jnp.concatenate([v, jnp.ones_like(v)], 1)
    even = soft_average(jnp.where(first, q, nothing), k, values_ones, mask)
    odd = soft_average(jnp.where(first, nothing, q), k, values_ones, mask)
    return jnp.where(first, even, odd).astype(BF16)


def block_scores(q, k):
    first = lanes_of_first(q.shape[0])
    nothing = jnp.zeros_like(q)
    keys = jnp.concatenate([jnp.where(first, k, nothing), jnp.where(first, nothing, k)], 0)
    return lax.dot_general(q, keys, (((1,), (1,)), ((), ())), preferred_element_type=F32)


def block_weights(scores, mask):
    weights = []
    for head in range(2):
        own = scores[:, head * 128 : (head + 1) * 128] + mask
        peak = jnp.max(own, axis=-1, keepdims=True)
        weights.append(jnp.exp2((own - peak) * LOG2_SCALE).astype(BF16))
    return jnp.concatenate(weights, 1)


def block_average(weights, v):
    first = lanes_of_first(v.shape[0])
    nothing, one = jnp.zeros_like(v), jnp.ones_like(v)
    values = jnp.concatenate(
        [
            jnp.concatenate([jnp.where(first, v, nothing), jnp.where(first, one, nothing)], 1),
            jnp.concatenate([jnp.where(first, nothing, v), jnp.where(first, nothing, one)], 1),
        ],
        0,
    )
    both = jnp.dot(weights, values, preferred_element_type=F32)
    return (both[:, :PAIR] / both[:, PAIR:]).astype(BF16)


def row_kernel(x_ref, *refs):
    slabs = refs[:8]
    part_hbm, wc_hbm, w, wo, qkv, attended, mask_ref, part, sems, sems_o, sems_part = refs[8:]
    copies = fetch_weights(slabs, 0, 768, w, sems)
    copies_out = fetch_weights(slabs, 768, 512, wo, sems_o)
    block = 256
    row = lax.broadcasted_iota(jnp.int32, (block, block), 0)
    col = lax.broadcasted_iota(jnp.int32, (block, block), 1)
    mask_ref[...] = jnp.where(col <= row, 0.0, -jnp.inf)
    for copy in copies:
        copy.wait()

    def project(i, _):
        at = pl.ds(pl.multiple_of(i * block, block), block)
        normed = normalized(x_ref[at, :].astype(F32))
        for half in range(2):
            made = jnp.dot(normed, w[half], preferred_element_type=F32).astype(BF16)
            for which in range(3):
                for p in range(2):
                    lane = which * 256 + p * PAIR
                    qkv[which, half * 2 + p, at, :] = made[:, lane : lane + PAIR]
        return 0

    lax.fori_loop(0, STRIDE // block, project, 0)

    for p in range(4):
        for i in range(STRIDE // block):
            upto = (i + 1) * block
            attended[i * block : upto, p * PAIR : (p + 1) * PAIR] = pair_attend(
                qkv[0, p, i * block : upto, :],
                qkv[1, p, :upto, :],
                qkv[2, p, :upto, :],
                mask_ref[...],
            )
    for copy in copies_out:
        copy.wait()

    copies = [pltpu.make_async_copy(wo.at[:, pl.ds(HALF, HALF), :], wc_hbm, sems.at[0])]
    copies[0].start()
    for i in range(STRIDE // block):
        at = slice(i * block, (i + 1) * block)
        for half in range(2):
            part[at, half * 512 : (half + 1) * 512] = jnp.dot(
                attended[at, :], wo[half, :HALF, :], preferred_element_type=F32
            )
        copies.append(pltpu.make_async_copy(part.at[at, :], part_hbm.at[at, :], sems_part.at[i]))
        copies[-1].start()
    for copy in copies:
        copy.wait()


def sequence_row(place):
    z = ((place >> 2) & 1) * 4 + ((place >> 3) & 1) * 2 + (place >> 4)
    return ((place >> 1) & 1) * 16 + z * 2 + (place & 1)


def place_of(row):
    z = ((row >> 1) & 1) * 4 + ((row >> 2) & 1) * 2 + ((row >> 3) & 1)
    return z * 4 + (row >> 4) * 2 + (row & 1)


WIDE = 16
STEP = 32 * WIDE


def one_hot(ref, lane_of):
    wanted = lane_of(lax.broadcasted_iota(jnp.int32, (STEP, 128), 0))
    lane = lax.broadcasted_iota(jnp.int32, (STEP, 128), 1)
    for at in range(0, STEP, 128):
        ref[:, at : at + 128] = jnp.where(wanted == lane + at, 1.0, 0.0).astype(BF16)


def col_kernel(x_hbm, *refs):
    o_hbm, x, w, out, mask_ref, sort_ref, back_ref, normed_ref, sems, sems_x, sems_o = refs[8:]
    steps = x.shape[1] // WIDE
    arrive, leave = [], []
    for i in range(steps):
        at = pl.ds(i * WIDE, WIDE)
        arrive.append(pltpu.make_async_copy(x_hbm.at[:, at, :], x.at[:, at, :], sems_x.at[i]))
        leave.append(pltpu.make_async_copy(out.at[:, at, :], o_hbm.at[:, at, :], sems_o.at[i]))
        arrive[i].start()
    weights = fetch_weights(refs[:8], 0, 768, w, sems)
    at = lax.broadcasted_iota(jnp.int32, (128, 128), 0)
    to = lax.broadcasted_iota(jnp.int32, (128, 128), 1)
    meets = jnp.logical_and(at // 32 == to // 32, to <= at)
    mask_ref[...] = jnp.where(meets, 0.0, -jnp.inf)
    one_hot(sort_ref, lambda new: place_of(new & 31) * WIDE + (new >> 5))
    one_hot(back_ref, lambda old: (old & (WIDE - 1)) * 32 + sequence_row(old >> 4))
    for i in range(steps):
        arrive[i].wait()
        taken = x[:, i * WIDE : (i + 1) * WIDE, :].reshape(STEP, D)
        for half in range(2):
            rows = slice(half * 256, half * 256 + 256)
            ordered = jnp.dot(sort_ref[rows, :], taken, preferred_element_type=F32)
            normed_ref[i * STEP + half * 256 : i * STEP + half * 256 + 256, :] = normalized(ordered)
    for copy in weights:
        copy.wait()
    for i in range(steps):
        attended = []
        for group in range(STEP // 256):
            start = i * STEP + group * 256
            parts = [
                jnp.dot(
                    normed_ref[start : start + 256, :], w[half], preferred_element_type=F32
                ).astype(BF16)
                for half in range(2)
            ]
            blocks = []
            for made in parts:
                for p in range(2):
                    for n in (0, 128):
                        blocks.append(
                            [
                                made[n : n + 128, which * 256 + p * PAIR : which * 256 + (p + 1) * PAIR]
                                for which in range(3)
                            ]
                        )
            scores = [block_scores(q, k) for q, k, _ in blocks]
            shares = [block_weights(score, mask_ref[...]) for score in scores]
            done = [block_average(share, v) for share, (_, _, v) in zip(shares, blocks)]
            attended.append(jnp.concatenate(
                [jnp.concatenate(done[n::2], 1) for n in range(2)], 0
            ))
        back = jnp.dot(
            back_ref[...], jnp.concatenate(attended, 0), preferred_element_type=F32
        ).astype(BF16)
        out[:, i * WIDE : (i + 1) * WIDE, :] = back.reshape(32, WIDE, HALF)
        leave[i].start()
    for copy in leave:
        copy.wait()


def out_kernel(part_hbm, col_hbm, w_hbm, o_hbm, part, col, w, out, sem_w, sems_p, sems_c, sems_o):
    block = 256
    weights = pltpu.make_async_copy(w_hbm, w, sem_w.at[0])
    weights.start()
    parts, cols, outs = [], [], []
    for i in range(STRIDE // block):
        at = pl.ds(i * block, block)
        parts.append(pltpu.make_async_copy(part_hbm.at[at, :], part.at[at, :], sems_p.at[i]))
        cols.append(pltpu.make_async_copy(col_hbm.at[at, :], col.at[at, :], sems_c.at[i]))
        outs.append(pltpu.make_async_copy(out.at[at, :], o_hbm.at[at, :], sems_o.at[i]))
        cols[i].start()
        parts[i].start()
    weights.wait()
    for i in range(STRIDE // block):
        at = slice(i * block, (i + 1) * block)
        cols[i].wait()
        parts[i].wait()
        for half in range(2):
            lanes = slice(half * 512, (half + 1) * 512)
            total = part[at, lanes] + jnp.dot(
                col[at, :], w[half], preferred_element_type=F32
            )
            out[at, lanes] = total.astype(BF16)
        outs[i].start()
    for copy in outs:
        copy.wait()


ANY = pl.BlockSpec(memory_space=pl.ANY)
WHOLE = pl.BlockSpec(memory_space=pltpu.VMEM)
FAR = pl.BlockSpec(memory_space=pltpu.HBM)
DMA = pltpu.SemaphoreType.DMA


def limit(mib):
    return pltpu.CompilerParams(vmem_limit_bytes=mib << 20)


def rebuilt_half(alpha_index, *parts):
    return pl.pallas_call(
        prep_kernel,
        out_shape=[
            jax.ShapeDtypeStruct((parts[0].shape[0], width), BF16) for width in (COLS, REST)
        ],
        in_specs=[pl.BlockSpec(memory_space=pltpu.SMEM)] + [WHOLE] * 4,
        out_specs=[WHOLE] * 2,
        compiler_params=limit(16),
        name="rebuilt_half",
    )(alpha_index, *parts)


def row_heads(sequence, slabs):
    return pl.pallas_call(
        row_kernel,
        out_shape=(
            jax.ShapeDtypeStruct((STRIDE, D), F32),
            jax.ShapeDtypeStruct((2, HALF, 512), BF16),
        ),
        in_specs=[WHOLE] + [ANY] * 8,
        out_specs=(FAR, FAR),
        scratch_shapes=[
            pltpu.VMEM((2, D, 768), BF16),
            pltpu.VMEM((2, D, 512), BF16),
            pltpu.VMEM((3, 4, STRIDE, PAIR), BF16),
            pltpu.VMEM((STRIDE, HALF), BF16),
            pltpu.VMEM((256, 256), F32),
            pltpu.VMEM((STRIDE, D), F32),
            DMA((16,)),
            DMA((16,)),
            DMA((4,)),
        ],
        compiler_params=limit(63),
        cost_estimate=pl.CostEstimate(
            flops=7_000_000_000, bytes_accessed=12 << 20, transcendentals=5_000_000
        ),
        name="row_heads",
    )(sequence, *slabs)


def col_heads(columns, slabs):
    rows, cols = columns.shape[:2]
    return pl.pallas_call(
        col_kernel,
        out_shape=jax.ShapeDtypeStruct((rows, cols, HALF), BF16),
        in_specs=[FAR] + [ANY] * 8,
        out_specs=FAR,
        scratch_shapes=[
            pltpu.VMEM((rows, cols, D), BF16),
            pltpu.VMEM((2, D, 768), BF16),
            pltpu.VMEM((rows, cols, HALF), BF16),
            pltpu.VMEM((128, 128), F32),
            pltpu.VMEM((STEP, STEP), BF16),
            pltpu.VMEM((STEP, STEP), BF16),
            pltpu.VMEM((rows * cols, D), BF16),
            DMA((16,)),
            DMA((cols // WIDE,)),
            DMA((cols // WIDE,)),
        ],
        compiler_params=limit(63),
        cost_estimate=pl.CostEstimate(
            flops=4_000_000_000, bytes_accessed=6 << 20, transcendentals=1_000_000
        ),
        name="col_heads",
    )(columns, *slabs)


def project_out(row_part, col_out, weights):
    return pl.pallas_call(
        out_kernel,
        out_shape=jax.ShapeDtypeStruct((STRIDE, D), BF16),
        in_specs=[FAR] * 3,
        out_specs=FAR,
        scratch_shapes=[
            pltpu.VMEM((STRIDE, D), F32),
            pltpu.VMEM((STRIDE, HALF), BF16),
            pltpu.VMEM((2, HALF, 512), BF16),
            pltpu.VMEM((STRIDE, D), BF16),
            DMA((1,)),
            DMA((4,)),
            DMA((4,)),
            DMA((4,)),
        ],
        compiler_params=limit(63),
        cost_estimate=pl.CostEstimate(
            flops=1_000_000_000, bytes_accessed=8 << 20, transcendentals=0
        ),
        name="project_out",
    )(row_part, col_out, weights)


ORDER = [sequence_row(place) for place in range(32)]


def exchange(blocks):
    return lax.all_to_all(
        blocks, "seq", split_axis=0, concat_axis=0, tiled=True, axis_index_groups=[ORDER]
    )


def with_far_y(own):
    return jnp.stack([own, send(own, hop(1, 0))])


def along_x(both):
    return [both] + [send(both, hop(0, dx)) for dx in range(1, 4)]


def both_cores(pieces):
    return pieces + [send(piece, CORE) for piece in pieces]


def shards(tokens, qkv_base, qkv_dir, out_base, out_dir, alpha_index):
    sequence = tokens[0]
    columns = exchange(sequence.reshape(32, 32, D))
    own_cols, own_rest = rebuilt_half(alpha_index, qkv_base, qkv_dir, out_base, out_dir)
    col_pieces = along_x(with_far_y(own_cols))
    rest_both, col_pieces = lax.optimization_barrier((with_far_y(own_rest), col_pieces))
    rest_pieces = along_x(rest_both)
    attended = col_heads(columns, both_cores(col_pieces))
    col_out = exchange(attended)
    rest_pieces, attended = lax.optimization_barrier((rest_pieces, attended))
    row_part, weights = row_heads(sequence, both_cores(rest_pieces))
    return project_out(row_part, col_out.reshape(STRIDE, HALF), weights)[None]


def solution(mesh):
    in_specs = (
        P("fsdp", "seq", None),
        P("fsdp", None),
        P("fsdp", None),
        P("fsdp", None),
        P("fsdp", None),
        P(),
    )
    out_specs = P("fsdp", "seq", None)
    return jax.shard_map(shards, mesh=mesh, in_specs=in_specs, out_specs=out_specs, check_vma=False)
```

```python
import math

import jax
import jax.numpy as jnp
from jax import lax
from jax.experimental import pallas as pl
from jax.experimental.pallas import tpu as pltpu
from jax.sharding import PartitionSpec as P

D = 1024
HEADS = 16
STRIDE = 1024
NALPHA = 1024
HEAD_DIM = D // HEADS
HALF = D // 2
PAIR = 2 * HEAD_DIM
COLS, REST = 768, 1280
F32, BF16 = jnp.float32, jnp.bfloat16
LOG2_SCALE = math.log2(math.e) / math.sqrt(HEAD_DIM)
BOTH = ("seq", "fsdp")


def split_index(i):
    s, f = divmod(i, 8)
    return s // 16, (s // 2) % 8, s % 2, f // 4, f % 4


def pairs(move):
    out = []
    for i in range(256):
        yl, z, c, yh, x = move(*split_index(i))
        out.append((i, ((yl * 8 + z) * 2 + c) * 8 + yh * 4 + x))
    return out


def hop(other_y, dx):
    return pairs(
        lambda yl, z, c, yh, x: (yl ^ other_y, z, c, yh ^ other_y, (x + dx) % 4)
    )


CORE = pairs(lambda yl, z, c, yh, x: (yl, z, 1 - c, yh, x))


def send(value, where):
    return lax.ppermute(value, BOTH, where)


def normalized(rows):
    mean_square = jnp.mean(rows * rows, axis=-1, keepdims=True)
    return (rows * lax.rsqrt(mean_square + 1e-06)).astype(BF16)


def fetch_weights(pieces, first, width, dest, sems):
    core = lax.axis_index("seq") % 2
    mine = lax.axis_index("fsdp")
    copies = []
    for n, (ref, start, other_core, other_y, dx) in enumerate(pieces):
        half = 1 - core if other_core else core
        y_hi = 1 - mine // 4 if other_y else mine // 4
        feature = pl.multiple_of((y_hi * 4 + (mine % 4 - dx + 4) % 4) * 128, 128)
        copy = pltpu.make_async_copy(
            ref.at[:, pl.ds(start + first, width)],
            dest.at[half, pl.ds(feature, 128), :],
            sems.at[n],
        )
        copy.start()
        copies.append(copy)
    return copies


def pieces_of(refs, start):
    return [
        (ref, 0 if n >= 8 else start, n % 8 >= 4, n >= 8, n % 4) for n, ref in enumerate(refs)
    ]


def prep_kernel(alpha_ref, qb_ref, qd_ref, ob_ref, od_ref, o_ref):
    core = lax.axis_index("seq") % 2
    step_alpha = (alpha_ref[0].astype(F32) + NALPHA) / (2.0 * NALPHA)
    at = 0
    for kind in (1, 0):
        for which in range(3):
            lanes = pl.ds(pl.multiple_of(which * D + kind * HALF + core * 256, 256), 256)
            rebuilt = qb_ref[:, lanes].astype(F32) + step_alpha * qd_ref[:, lanes].astype(F32)
            o_ref[:, at : at + 256] = rebuilt.astype(BF16)
            at += 256
    lanes = pl.ds(pl.multiple_of(core * 512, 512), 512)
    rebuilt = ob_ref[:, lanes].astype(F32) + step_alpha * od_ref[:, lanes].astype(F32)
    o_ref[:, at:] = rebuilt.astype(BF16)


def soft_average(queries, keys, values_ones, mask):
    scores = lax.dot_general(queries, keys, (((1,), (1,)), ((), ())), preferred_element_type=F32)
    width = mask.shape[1]
    last = scores[:, -width:] + mask
    scores = last if width == scores.shape[1] else jnp.concatenate([scores[:, :-width], last], 1)
    peak = jnp.max(scores, axis=-1, keepdims=True)
    weights = jnp.exp2((scores - peak) * LOG2_SCALE).astype(BF16)
    both = jnp.dot(weights, values_ones, preferred_element_type=F32)
    return both[:, :PAIR] / both[:, PAIR:]


def lanes_of_first(rows):
    return lax.broadcasted_iota(jnp.int32, (rows, PAIR), 1) < HEAD_DIM


def pair_attend(q, k, v, mask):
    first = lanes_of_first(q.shape[0])
    nothing = jnp.zeros_like(q)
    values_ones = jnp.concatenate([v, jnp.ones_like(v)], 1)
    even = soft_average(jnp.where(first, q, nothing), k, values_ones, mask)
    odd = soft_average(jnp.where(first, nothing, q), k, values_ones, mask)
    return jnp.where(first, even, odd).astype(BF16)


def block_scores(q, k):
    first = lanes_of_first(q.shape[0])
    nothing = jnp.zeros_like(q)
    keys = jnp.concatenate([jnp.where(first, k, nothing), jnp.where(first, nothing, k)], 0)
    return lax.dot_general(q, keys, (((1,), (1,)), ((), ())), preferred_element_type=F32)


def block_weights(scores, mask):
    weights = []
    for head in range(2):
        own = scores[:, head * 128 : (head + 1) * 128] + mask
        peak = jnp.max(own, axis=-1, keepdims=True)
        weights.append(jnp.exp2((own - peak) * LOG2_SCALE).astype(BF16))
    return jnp.concatenate(weights, 1)


def block_average(weights, v):
    first = lanes_of_first(v.shape[0])
    nothing, one = jnp.zeros_like(v), jnp.ones_like(v)
    values = jnp.concatenate(
        [
            jnp.concatenate([jnp.where(first, v, nothing), jnp.where(first, one, nothing)], 1),
            jnp.concatenate([jnp.where(first, nothing, v), jnp.where(first, nothing, one)], 1),
        ],
        0,
    )
    both = jnp.dot(weights, values, preferred_element_type=F32)
    return (both[:, :PAIR] / both[:, PAIR:]).astype(BF16)


def row_kernel(x_ref, *refs):
    pieces = pieces_of(refs[:16], COLS)
    part_hbm, wc_hbm, w, wo, qkv, attended, mask_ref, part, sems, sems_o, sems_part = refs[16:]
    copies = fetch_weights(pieces, 0, 768, w, sems)
    copies_out = fetch_weights(pieces, 768, 512, wo, sems_o)
    block = 256
    row = lax.broadcasted_iota(jnp.int32, (block, block), 0)
    col = lax.broadcasted_iota(jnp.int32, (block, block), 1)
    mask_ref[...] = jnp.where(col <= row, 0.0, -jnp.inf)
    for copy in copies:
        copy.wait()

    def project(i, _):
        at = pl.ds(pl.multiple_of(i * block, block), block)
        normed = normalized(x_ref[at, :].astype(F32))
        for half in range(2):
            made = jnp.dot(normed, w[half], preferred_element_type=F32).astype(BF16)
            for which in range(3):
                for p in range(2):
                    lane = which * 256 + p * PAIR
                    qkv[which, half * 2 + p, at, :] = made[:, lane : lane + PAIR]
        return 0

    lax.fori_loop(0, STRIDE // block, project, 0)

    for p in range(4):
        for i in range(STRIDE // block):
            upto = (i + 1) * block
            attended[i * block : upto, p * PAIR : (p + 1) * PAIR] = pair_attend(
                qkv[0, p, i * block : upto, :],
                qkv[1, p, :upto, :],
                qkv[2, p, :upto, :],
                mask_ref[...],
            )
    for copy in copies_out:
        copy.wait()

    copies = [pltpu.make_async_copy(wo.at[:, pl.ds(HALF, HALF), :], wc_hbm, sems.at[0])]
    copies[0].start()
    for i in range(STRIDE // block):
        at = slice(i * block, (i + 1) * block)
        for half in range(2):
            part[at, half * 512 : (half + 1) * 512] = jnp.dot(
                attended[at, :], wo[half, :HALF, :], preferred_element_type=F32
            )
        copies.append(pltpu.make_async_copy(part.at[at, :], part_hbm.at[at, :], sems_part.at[i]))
        copies[-1].start()
    for copy in copies:
        copy.wait()


def sequence_row(place):
    z = ((place >> 2) & 1) * 4 + ((place >> 3) & 1) * 2 + (place >> 4)
    return ((place >> 1) & 1) * 16 + z * 2 + (place & 1)


def place_of(row):
    z = ((row >> 1) & 1) * 4 + ((row >> 2) & 1) * 2 + ((row >> 3) & 1)
    return z * 4 + (row >> 4) * 2 + (row & 1)


WIDE = 16
STEP = 32 * WIDE


def one_hot(ref, lane_of):
    wanted = lane_of(lax.broadcasted_iota(jnp.int32, (STEP, 128), 0))
    lane = lax.broadcasted_iota(jnp.int32, (STEP, 128), 1)
    for at in range(0, STEP, 128):
        ref[:, at : at + 128] = jnp.where(wanted == lane + at, 1.0, 0.0).astype(BF16)


def col_kernel(x_hbm, *refs):
    o_hbm, x, w, out, mask_ref, sort_ref, back_ref, normed_ref, sems, sems_x, sems_o = refs[16:]
    steps = x.shape[1] // WIDE
    arrive, leave = [], []
    for i in range(steps):
        at = pl.ds(i * WIDE, WIDE)
        arrive.append(pltpu.make_async_copy(x_hbm.at[:, at, :], x.at[:, at, :], sems_x.at[i]))
        leave.append(pltpu.make_async_copy(out.at[:, at, :], o_hbm.at[:, at, :], sems_o.at[i]))
        arrive[i].start()
    weights = fetch_weights(pieces_of(refs[:16], 0), 0, 768, w, sems)
    at = lax.broadcasted_iota(jnp.int32, (128, 128), 0)
    to = lax.broadcasted_iota(jnp.int32, (128, 128), 1)
    meets = jnp.logical_and(at // 32 == to // 32, to <= at)
    mask_ref[...] = jnp.where(meets, 0.0, -jnp.inf)
    one_hot(sort_ref, lambda new: place_of(new & 31) * WIDE + (new >> 5))
    one_hot(back_ref, lambda old: (old & (WIDE - 1)) * 32 + sequence_row(old >> 4))
    for i in range(steps):
        arrive[i].wait()
        taken = x[:, i * WIDE : (i + 1) * WIDE, :].reshape(STEP, D)
        for half in range(2):
            rows = slice(half * 256, half * 256 + 256)
            ordered = jnp.dot(sort_ref[rows, :], taken, preferred_element_type=F32)
            normed_ref[i * STEP + half * 256 : i * STEP + half * 256 + 256, :] = normalized(ordered)
    for copy in weights:
        copy.wait()
    for i in range(steps):
        attended = []
        for group in range(STEP // 256):
            start = i * STEP + group * 256
            parts = [
                jnp.dot(
                    normed_ref[start : start + 256, :], w[half], preferred_element_type=F32
                ).astype(BF16)
                for half in range(2)
            ]
            blocks = []
            for made in parts:
                for p in range(2):
                    for n in (0, 128):
                        blocks.append(
                            [
                                made[n : n + 128, which * 256 + p * PAIR : which * 256 + (p + 1) * PAIR]
                                for which in range(3)
                            ]
                        )
            scores = [block_scores(q, k) for q, k, _ in blocks]
            shares = [block_weights(score, mask_ref[...]) for score in scores]
            done = [block_average(share, v) for share, (_, _, v) in zip(shares, blocks)]
            attended.append(jnp.concatenate(
                [jnp.concatenate(done[n::2], 1) for n in range(2)], 0
            ))
        back = jnp.dot(
            back_ref[...], jnp.concatenate(attended, 0), preferred_element_type=F32
        ).astype(BF16)
        out[:, i * WIDE : (i + 1) * WIDE, :] = back.reshape(32, WIDE, HALF)
        leave[i].start()
    for copy in leave:
        copy.wait()


def out_kernel(part_hbm, col_hbm, w_hbm, o_hbm, part, col, w, out, sem_w, sems_p, sems_c, sems_o):
    block = 256
    weights = pltpu.make_async_copy(w_hbm, w, sem_w.at[0])
    weights.start()
    parts, cols, outs = [], [], []
    for i in range(STRIDE // block):
        at = pl.ds(i * block, block)
        parts.append(pltpu.make_async_copy(part_hbm.at[at, :], part.at[at, :], sems_p.at[i]))
        cols.append(pltpu.make_async_copy(col_hbm.at[at, :], col.at[at, :], sems_c.at[i]))
        outs.append(pltpu.make_async_copy(out.at[at, :], o_hbm.at[at, :], sems_o.at[i]))
        cols[i].start()
        parts[i].start()
    weights.wait()
    for i in range(STRIDE // block):
        at = slice(i * block, (i + 1) * block)
        cols[i].wait()
        parts[i].wait()
        for half in range(2):
            lanes = slice(half * 512, (half + 1) * 512)
            total = part[at, lanes] + jnp.dot(
                col[at, :], w[half], preferred_element_type=F32
            )
            out[at, lanes] = total.astype(BF16)
        outs[i].start()
    for copy in outs:
        copy.wait()


ANY = pl.BlockSpec(memory_space=pl.ANY)
WHOLE = pl.BlockSpec(memory_space=pltpu.VMEM)
FAR = pl.BlockSpec(memory_space=pltpu.HBM)
DMA = pltpu.SemaphoreType.DMA


def limit(mib):
    return pltpu.CompilerParams(vmem_limit_bytes=mib << 20)


def rebuilt_half(alpha_index, *parts):
    return pl.pallas_call(
        prep_kernel,
        out_shape=jax.ShapeDtypeStruct((parts[0].shape[0], COLS + REST), BF16),
        in_specs=[pl.BlockSpec(memory_space=pltpu.SMEM)] + [WHOLE] * 4,
        out_specs=WHOLE,
        compiler_params=limit(16),
        name="rebuilt_half",
    )(alpha_index, *parts)


def row_heads(sequence, slabs):
    return pl.pallas_call(
        row_kernel,
        out_shape=(
            jax.ShapeDtypeStruct((STRIDE, D), F32),
            jax.ShapeDtypeStruct((2, HALF, 512), BF16),
        ),
        in_specs=[WHOLE] + [ANY] * 16,
        out_specs=(FAR, FAR),
        scratch_shapes=[
            pltpu.VMEM((2, D, 768), BF16),
            pltpu.VMEM((2, D, 512), BF16),
            pltpu.VMEM((3, 4, STRIDE, PAIR), BF16),
            pltpu.VMEM((STRIDE, HALF), BF16),
            pltpu.VMEM((256, 256), F32),
            pltpu.VMEM((STRIDE, D), F32),
            DMA((16,)),
            DMA((16,)),
            DMA((4,)),
        ],
        compiler_params=limit(63),
        cost_estimate=pl.CostEstimate(
            flops=7_000_000_000, bytes_accessed=12 << 20, transcendentals=5_000_000
        ),
        name="row_heads",
    )(sequence, *slabs)


def col_heads(columns, slabs):
    rows, cols = columns.shape[:2]
    return pl.pallas_call(
        col_kernel,
        out_shape=jax.ShapeDtypeStruct((rows, cols, HALF), BF16),
        in_specs=[FAR] + [ANY] * 16,
        out_specs=FAR,
        scratch_shapes=[
            pltpu.VMEM((rows, cols, D), BF16),
            pltpu.VMEM((2, D, 768), BF16),
            pltpu.VMEM((rows, cols, HALF), BF16),
            pltpu.VMEM((128, 128), F32),
            pltpu.VMEM((STEP, STEP), BF16),
            pltpu.VMEM((STEP, STEP), BF16),
            pltpu.VMEM((rows * cols, D), BF16),
            DMA((16,)),
            DMA((cols // WIDE,)),
            DMA((cols // WIDE,)),
        ],
        compiler_params=limit(63),
        cost_estimate=pl.CostEstimate(
            flops=4_000_000_000, bytes_accessed=6 << 20, transcendentals=1_000_000
        ),
        name="col_heads",
    )(columns, *slabs)


def project_out(row_part, col_out, weights):
    return pl.pallas_call(
        out_kernel,
        out_shape=jax.ShapeDtypeStruct((STRIDE, D), BF16),
        in_specs=[FAR] * 3,
        out_specs=FAR,
        scratch_shapes=[
            pltpu.VMEM((STRIDE, D), F32),
            pltpu.VMEM((STRIDE, HALF), BF16),
            pltpu.VMEM((2, HALF, 512), BF16),
            pltpu.VMEM((STRIDE, D), BF16),
            DMA((1,)),
            DMA((4,)),
            DMA((4,)),
            DMA((4,)),
        ],
        compiler_params=limit(63),
        cost_estimate=pl.CostEstimate(
            flops=1_000_000_000, bytes_accessed=8 << 20, transcendentals=0
        ),
        name="project_out",
    )(row_part, col_out, weights)


ORDER = [sequence_row(place) for place in range(32)]


def exchange(blocks):
    return lax.all_to_all(
        blocks, "seq", split_axis=0, concat_axis=0, tiled=True, axis_index_groups=[ORDER]
    )


def along_x(piece):
    return [piece] + [send(piece, hop(0, dx)) for dx in range(1, 4)]


def across_y(pieces):
    return [send(piece, hop(1, 0)) for piece in pieces]


def both_cores(pieces):
    return pieces + [send(piece, CORE) for piece in pieces]


def shards(tokens, qkv_base, qkv_dir, out_base, out_dir, alpha_index):
    sequence = tokens[0]
    columns = exchange(sequence.reshape(32, 32, D))
    own = rebuilt_half(alpha_index, qkv_base, qkv_dir, out_base, out_dir)
    (far_cols,) = across_y([own[:, :COLS]])
    near = along_x(own)
    far_cols = both_cores(along_x(far_cols))
    far_rest = across_y([piece[:, COLS:] for piece in near])
    near = both_cores(near)
    attended = col_heads(columns, near + far_cols)
    far_rest, attended = lax.optimization_barrier((far_rest, attended))
    col_out = exchange(attended)
    row_part, weights = row_heads(sequence, near + both_cores(far_rest))
    return project_out(row_part, col_out.reshape(STRIDE, HALF), weights)[None]


def solution(mesh):
    in_specs = (
        P("fsdp", "seq", None),
        P("fsdp", None),
        P("fsdp", None),
        P("fsdp", None),
        P("fsdp", None),
        P(),
    )
    out_specs = P("fsdp", "seq", None)
    return jax.shard_map(shards, mesh=mesh, in_specs=in_specs, out_specs=out_specs, check_vma=False)
```

```python
import math

import jax
import jax.numpy as jnp
from jax import lax
from jax.experimental import pallas as pl
from jax.experimental.pallas import tpu as pltpu
from jax.sharding import PartitionSpec as P

D = 1024
HEADS = 16
STRIDE = 1024
NALPHA = 1024
HEAD_DIM = D // HEADS
HALF = D // 2
PAIR = 2 * HEAD_DIM
QKV, OUT = 768, 512
F32, BF16 = jnp.float32, jnp.bfloat16
LOG2_SCALE = math.log2(math.e) / math.sqrt(HEAD_DIM)
BOTH = ("seq", "fsdp")


def split_index(i):
    s, f = divmod(i, 8)
    return s // 16, (s // 2) % 8, s % 2, f // 4, f % 4


def pairs(move):
    out = []
    for i in range(256):
        yl, z, c, yh, x = move(*split_index(i))
        out.append((i, ((yl * 8 + z) * 2 + c) * 8 + yh * 4 + x))
    return out


def hop(other_y, dx):
    return pairs(
        lambda yl, z, c, yh, x: (yl ^ other_y, z, c, yh ^ other_y, (x + dx) % 4)
    )


CORE = pairs(lambda yl, z, c, yh, x: (yl, z, 1 - c, yh, x))


def send(value, where):
    return lax.ppermute(value, BOTH, where)


def normalized(rows):
    mean_square = jnp.mean(rows * rows, axis=-1, keepdims=True)
    return (rows * lax.rsqrt(mean_square + 1e-06)).astype(BF16)


def fetch_weights(slabs, dest, sems):
    core = lax.axis_index("seq") % 2
    mine = lax.axis_index("fsdp")
    copies = []
    for n, slab in enumerate(slabs):
        half = core if n < 4 else 1 - core
        for k in range(2):
            y_hi = mine // 4 if k == 0 else 1 - mine // 4
            feature = pl.multiple_of((y_hi * 4 + (mine % 4 - n % 4 + 4) % 4) * 128, 128)
            copy = pltpu.make_async_copy(
                slab.at[k],
                dest.at[half, pl.ds(feature, 128), :],
                sems.at[n * 2 + k],
            )
            copy.start()
            copies.append(copy)
    return copies


def prep_kernel(alpha_ref, qb_ref, qd_ref, ob_ref, od_ref, cols_ref, rest_ref):
    core = lax.axis_index("seq") % 2
    step_alpha = (alpha_ref[0].astype(F32) + NALPHA) / (2.0 * NALPHA)
    for kind, to_ref in ((1, cols_ref), (0, rest_ref)):
        for which in range(3):
            lanes = pl.ds(pl.multiple_of(which * D + kind * HALF + core * 256, 256), 256)
            rebuilt = qb_ref[:, lanes].astype(F32) + step_alpha * qd_ref[:, lanes].astype(F32)
            to_ref[:, which * 256 : (which + 1) * 256] = rebuilt.astype(BF16)
    lanes = pl.ds(pl.multiple_of(core * 512, 512), 512)
    rebuilt = ob_ref[:, lanes].astype(F32) + step_alpha * od_ref[:, lanes].astype(F32)
    rest_ref[:, 768:] = rebuilt.astype(BF16)


def soft_average(queries, keys, values_ones, mask):
    scores = lax.dot_general(queries, keys, (((1,), (1,)), ((), ())), preferred_element_type=F32)
    width = mask.shape[1]
    last = scores[:, -width:] + mask
    scores = last if width == scores.shape[1] else jnp.concatenate([scores[:, :-width], last], 1)
    peak = jnp.max(scores, axis=-1, keepdims=True)
    weights = jnp.exp2((scores - peak) * LOG2_SCALE).astype(BF16)
    both = jnp.dot(weights, values_ones, preferred_element_type=F32)
    return both[:, :PAIR] / both[:, PAIR:]


def lanes_of_first(rows):
    return lax.broadcasted_iota(jnp.int32, (rows, PAIR), 1) < HEAD_DIM


def pair_attend(q, k, v, mask):
    first = lanes_of_first(q.shape[0])
    nothing = jnp.zeros_like(q)
    values_ones = jnp.concatenate([v, jnp.ones_like(v)], 1)
    even = soft_average(jnp.where(first, q, nothing), k, values_ones, mask)
    odd = soft_average(jnp.where(first, nothing, q), k, values_ones, mask)
    return jnp.where(first, even, odd).astype(BF16)


def block_scores(q, k):
    first = lanes_of_first(q.shape[0])
    nothing = jnp.zeros_like(q)
    keys = jnp.concatenate([jnp.where(first, k, nothing), jnp.where(first, nothing, k)], 0)
    return lax.dot_general(q, keys, (((1,), (1,)), ((), ())), preferred_element_type=F32)


def block_weights(scores, mask):
    weights = []
    for head in range(2):
        own = scores[:, head * 128 : (head + 1) * 128] + mask
        peak = jnp.max(own, axis=-1, keepdims=True)
        weights.append(jnp.exp2((own - peak) * LOG2_SCALE).astype(BF16))
    return jnp.concatenate(weights, 1)


def block_average(weights, v):
    first = lanes_of_first(v.shape[0])
    nothing, one = jnp.zeros_like(v), jnp.ones_like(v)
    values = jnp.concatenate(
        [
            jnp.concatenate([jnp.where(first, v, nothing), jnp.where(first, one, nothing)], 1),
            jnp.concatenate([jnp.where(first, nothing, v), jnp.where(first, nothing, one)], 1),
        ],
        0,
    )
    both = jnp.dot(weights, values, preferred_element_type=F32)
    return (both[:, :PAIR] / both[:, PAIR:]).astype(BF16)


def row_kernel(x_ref, *refs):
    slabs = refs[:8]
    o_hbm, w, qkv, attended, mask_ref, sems, sems_o = refs[8:]
    copies = fetch_weights(slabs, w, sems)
    block = 256
    row = lax.broadcasted_iota(jnp.int32, (block, block), 0)
    col = lax.broadcasted_iota(jnp.int32, (block, block), 1)
    mask_ref[...] = jnp.where(col <= row, 0.0, -jnp.inf)
    for copy in copies:
        copy.wait()

    def project(i, _):
        at = pl.ds(pl.multiple_of(i * block, block), block)
        normed = normalized(x_ref[at, :].astype(F32))
        for half in range(2):
            made = jnp.dot(normed, w[half], preferred_element_type=F32).astype(BF16)
            for which in range(3):
                for p in range(2):
                    lane = which * 256 + p * PAIR
                    qkv[which, half * 2 + p, at, :] = made[:, lane : lane + PAIR]
        return 0

    lax.fori_loop(0, STRIDE // block, project, 0)

    for p in range(4):
        for i in range(STRIDE // block):
            upto = (i + 1) * block
            attended[i * block : upto, p * PAIR : (p + 1) * PAIR] = pair_attend(
                qkv[0, p, i * block : upto, :],
                qkv[1, p, :upto, :],
                qkv[2, p, :upto, :],
                mask_ref[...],
            )
    copy = pltpu.make_async_copy(attended, o_hbm, sems_o.at[0])
    copy.start()
    copy.wait()


def sequence_row(place):
    z = ((place >> 2) & 1) * 4 + ((place >> 3) & 1) * 2 + (place >> 4)
    return ((place >> 1) & 1) * 16 + z * 2 + (place & 1)


def place_of(row):
    z = ((row >> 1) & 1) * 4 + ((row >> 2) & 1) * 2 + ((row >> 3) & 1)
    return z * 4 + (row >> 4) * 2 + (row & 1)


WIDE = 16
STEP = 32 * WIDE


def one_hot(ref, lane_of):
    wanted = lane_of(lax.broadcasted_iota(jnp.int32, (STEP, 128), 0))
    lane = lax.broadcasted_iota(jnp.int32, (STEP, 128), 1)
    for at in range(0, STEP, 128):
        ref[:, at : at + 128] = jnp.where(wanted == lane + at, 1.0, 0.0).astype(BF16)


def col_kernel(x_hbm, *refs):
    o_hbm, x, w, out, mask_ref, sort_ref, back_ref, normed_ref, sems, sems_x, sems_o = refs[8:]
    steps = x.shape[1] // WIDE
    arrive, leave = [], []
    for i in range(steps):
        at = pl.ds(i * WIDE, WIDE)
        arrive.append(pltpu.make_async_copy(x_hbm.at[:, at, :], x.at[:, at, :], sems_x.at[i]))
        leave.append(pltpu.make_async_copy(out.at[:, at, :], o_hbm.at[:, at, :], sems_o.at[i]))
        arrive[i].start()
    weights = fetch_weights(refs[:8], w, sems)
    at = lax.broadcasted_iota(jnp.int32, (128, 128), 0)
    to = lax.broadcasted_iota(jnp.int32, (128, 128), 1)
    meets = jnp.logical_and(at // 32 == to // 32, to <= at)
    mask_ref[...] = jnp.where(meets, 0.0, -jnp.inf)
    one_hot(sort_ref, lambda new: place_of(new & 31) * WIDE + (new >> 5))
    one_hot(back_ref, lambda old: (old & (WIDE - 1)) * 32 + sequence_row(old >> 4))
    for i in range(steps):
        arrive[i].wait()
        taken = x[:, i * WIDE : (i + 1) * WIDE, :].reshape(STEP, D)
        for half in range(2):
            rows = slice(half * 256, half * 256 + 256)
            ordered = jnp.dot(sort_ref[rows, :], taken, preferred_element_type=F32)
            normed_ref[i * STEP + half * 256 : i * STEP + half * 256 + 256, :] = normalized(ordered)
    for copy in weights:
        copy.wait()
    for i in range(steps):
        attended = []
        for group in range(STEP // 256):
            start = i * STEP + group * 256
            parts = [
                jnp.dot(
                    normed_ref[start : start + 256, :], w[half], preferred_element_type=F32
                ).astype(BF16)
                for half in range(2)
            ]
            blocks = []
            for made in parts:
                for p in range(2):
                    for n in (0, 128):
                        blocks.append(
                            [
                                made[n : n + 128, which * 256 + p * PAIR : which * 256 + (p + 1) * PAIR]
                                for which in range(3)
                            ]
                        )
            scores = [block_scores(q, k) for q, k, _ in blocks]
            shares = [block_weights(score, mask_ref[...]) for score in scores]
            done = [block_average(share, v) for share, (_, _, v) in zip(shares, blocks)]
            attended.append(jnp.concatenate(
                [jnp.concatenate(done[n::2], 1) for n in range(2)], 0
            ))
        back = jnp.dot(
            back_ref[...], jnp.concatenate(attended, 0), preferred_element_type=F32
        ).astype(BF16)
        out[:, i * WIDE : (i + 1) * WIDE, :] = back.reshape(32, WIDE, HALF)
        leave[i].start()
    for copy in leave:
        copy.wait()


def out_kernel(row_hbm, col_hbm, *refs):
    o_hbm, row, col, w, out, sems, sems_r, sems_c, sems_o = refs[8:]
    block = 256
    weights = fetch_weights(refs[:8], w, sems)
    rows, cols, outs = [], [], []
    for i in range(STRIDE // block):
        at = pl.ds(i * block, block)
        rows.append(pltpu.make_async_copy(row_hbm.at[at, :], row.at[at, :], sems_r.at[i]))
        cols.append(pltpu.make_async_copy(col_hbm.at[at, :], col.at[at, :], sems_c.at[i]))
        outs.append(pltpu.make_async_copy(out.at[at, :], o_hbm.at[at, :], sems_o.at[i]))
        rows[i].start()
        cols[i].start()
    for copy in weights:
        copy.wait()
    for i in range(STRIDE // block):
        at = slice(i * block, (i + 1) * block)
        rows[i].wait()
        cols[i].wait()
        for half in range(2):
            total = jnp.dot(row[at, :], w[half, :HALF, :], preferred_element_type=F32)
            total += jnp.dot(col[at, :], w[half, HALF:, :], preferred_element_type=F32)
            out[at, half * 512 : (half + 1) * 512] = total.astype(BF16)
        outs[i].start()
    for copy in outs:
        copy.wait()


ANY = pl.BlockSpec(memory_space=pl.ANY)
WHOLE = pl.BlockSpec(memory_space=pltpu.VMEM)
FAR = pl.BlockSpec(memory_space=pltpu.HBM)
DMA = pltpu.SemaphoreType.DMA


def limit(mib):
    return pltpu.CompilerParams(vmem_limit_bytes=mib << 20)


def rebuilt_half(alpha_index, *parts):
    return pl.pallas_call(
        prep_kernel,
        out_shape=[
            jax.ShapeDtypeStruct((parts[0].shape[0], width), BF16) for width in (QKV, QKV + OUT)
        ],
        in_specs=[pl.BlockSpec(memory_space=pltpu.SMEM)] + [WHOLE] * 4,
        out_specs=[WHOLE] * 2,
        compiler_params=limit(16),
        name="rebuilt_half",
    )(alpha_index, *parts)


def row_heads(sequence, slabs):
    return pl.pallas_call(
        row_kernel,
        out_shape=jax.ShapeDtypeStruct((STRIDE, HALF), BF16),
        in_specs=[WHOLE] + [ANY] * 8,
        out_specs=FAR,
        scratch_shapes=[
            pltpu.VMEM((2, D, QKV), BF16),
            pltpu.VMEM((3, 4, STRIDE, PAIR), BF16),
            pltpu.VMEM((STRIDE, HALF), BF16),
            pltpu.VMEM((256, 256), F32),
            DMA((16,)),
            DMA((1,)),
        ],
        compiler_params=limit(63),
        cost_estimate=pl.CostEstimate(
            flops=6_000_000_000, bytes_accessed=6 << 20, transcendentals=5_000_000
        ),
        name="row_heads",
    )(sequence, *slabs)


def col_heads(columns, slabs):
    rows, cols = columns.shape[:2]
    return pl.pallas_call(
        col_kernel,
        out_shape=jax.ShapeDtypeStruct((rows, cols, HALF), BF16),
        in_specs=[FAR] + [ANY] * 8,
        out_specs=FAR,
        scratch_shapes=[
            pltpu.VMEM((rows, cols, D), BF16),
            pltpu.VMEM((2, D, QKV), BF16),
            pltpu.VMEM((rows, cols, HALF), BF16),
            pltpu.VMEM((128, 128), F32),
            pltpu.VMEM((STEP, STEP), BF16),
            pltpu.VMEM((STEP, STEP), BF16),
            pltpu.VMEM((rows * cols, D), BF16),
            DMA((16,)),
            DMA((cols // WIDE,)),
            DMA((cols // WIDE,)),
        ],
        compiler_params=limit(63),
        cost_estimate=pl.CostEstimate(
            flops=4_000_000_000, bytes_accessed=6 << 20, transcendentals=1_000_000
        ),
        name="col_heads",
    )(columns, *slabs)


def project_out(row_out, col_out, slabs):
    return pl.pallas_call(
        out_kernel,
        out_shape=jax.ShapeDtypeStruct((STRIDE, D), BF16),
        in_specs=[FAR] * 2 + [ANY] * 8,
        out_specs=FAR,
        scratch_shapes=[
            pltpu.VMEM((STRIDE, HALF), BF16),
            pltpu.VMEM((STRIDE, HALF), BF16),
            pltpu.VMEM((2, D, OUT), BF16),
            pltpu.VMEM((STRIDE, D), BF16),
            DMA((16,)),
            DMA((4,)),
            DMA((4,)),
            DMA((4,)),
        ],
        compiler_params=limit(63),
        cost_estimate=pl.CostEstimate(
            flops=2_000_000_000, bytes_accessed=6 << 20, transcendentals=0
        ),
        name="project_out",
    )(row_out, col_out, *slabs)


ORDER = [sequence_row(place) for place in range(32)]


def exchange(blocks):
    return lax.all_to_all(
        blocks, "seq", split_axis=0, concat_axis=0, tiled=True, axis_index_groups=[ORDER]
    )


def with_far_y(own):
    return jnp.stack([own, send(own, hop(1, 0))])


def along_x(both):
    return [both] + [send(both, hop(0, dx)) for dx in range(1, 4)]


def both_cores(pieces):
    return pieces + [send(piece, CORE) for piece in pieces]


def shards(tokens, qkv_base, qkv_dir, out_base, out_dir, alpha_index):
    sequence = tokens[0]
    columns = exchange(sequence.reshape(32, 32, D))
    own_cols, own_rest = rebuilt_half(alpha_index, qkv_base, qkv_dir, out_base, out_dir)
    col_pieces = along_x(with_far_y(own_cols))
    rest, col_pieces = lax.optimization_barrier((with_far_y(own_rest), col_pieces))
    row_pieces = along_x(rest[:, :, :QKV])
    attended = col_heads(columns, both_cores(col_pieces))
    row_pieces, rest, attended = lax.optimization_barrier((row_pieces, rest, attended))
    col_out = exchange(attended)
    out_pieces = along_x(rest[:, :, QKV:])
    row_out = row_heads(sequence, both_cores(row_pieces))
    out_pieces, row_out = lax.optimization_barrier((out_pieces, row_out))
    return project_out(row_out, col_out.reshape(STRIDE, HALF), both_cores(out_pieces))[None]


def solution(mesh):
    in_specs = (
        P("fsdp", "seq", None),
        P("fsdp", None),
        P("fsdp", None),
        P("fsdp", None),
        P("fsdp", None),
        P(),
    )
    out_specs = P("fsdp", "seq", None)
    return jax.shard_map(shards, mesh=mesh, in_specs=in_specs, out_specs=out_specs, check_vma=False)
```

```python
import math

import jax
import jax.numpy as jnp
from jax import lax
from jax.experimental import pallas as pl
from jax.experimental.pallas import tpu as pltpu
from jax.sharding import PartitionSpec as P

D = 1024
HEADS = 16
STRIDE = 1024
NALPHA = 1024
HEAD_DIM = D // HEADS
HALF = D // 2
PAIR = 2 * HEAD_DIM
QKV, OUT = 768, 512
F32, BF16 = jnp.float32, jnp.bfloat16
LOG2_SCALE = math.log2(math.e) / math.sqrt(HEAD_DIM)
BOTH = ("seq", "fsdp")


def split_index(i):
    s, f = divmod(i, 8)
    return s // 16, (s // 2) % 8, s % 2, f // 4, f % 4


def pairs(move):
    out = []
    for i in range(256):
        yl, z, c, yh, x = move(*split_index(i))
        out.append((i, ((yl * 8 + z) * 2 + c) * 8 + yh * 4 + x))
    return out


def hop(other_y, dx):
    return pairs(
        lambda yl, z, c, yh, x: (yl ^ other_y, z, c, yh ^ other_y, (x + dx) % 4)
    )


CORE = pairs(lambda yl, z, c, yh, x: (yl, z, 1 - c, yh, x))


def send(value, where):
    return lax.ppermute(value, BOTH, where)


def normalized(rows):
    mean_square = jnp.mean(rows * rows, axis=-1, keepdims=True)
    return (rows * lax.rsqrt(mean_square + 1e-06)).astype(BF16)


def fetch_weights(slabs, dest, sems):
    core = lax.axis_index("seq") % 2
    mine = lax.axis_index("fsdp")
    copies = []
    for n, slab in enumerate(slabs):
        half = core if n < 4 else 1 - core
        for k in range(2):
            y_hi = mine // 4 if k == 0 else 1 - mine // 4
            feature = pl.multiple_of((y_hi * 4 + (mine % 4 - n % 4 + 4) % 4) * 128, 128)
            copy = pltpu.make_async_copy(
                slab.at[k],
                dest.at[half, pl.ds(feature, 128), :],
                sems.at[n * 2 + k],
            )
            copy.start()
            copies.append(copy)
    return copies


def prep_kernel(alpha_ref, qb_ref, qd_ref, ob_ref, od_ref, cols_ref, rest_ref):
    core = lax.axis_index("seq") % 2
    step_alpha = (alpha_ref[0].astype(F32) + NALPHA) / (2.0 * NALPHA)
    for kind, to_ref in ((1, cols_ref), (0, rest_ref)):
        for which in range(3):
            lanes = pl.ds(pl.multiple_of(which * D + kind * HALF + core * 256, 256), 256)
            rebuilt = qb_ref[:, lanes].astype(F32) + step_alpha * qd_ref[:, lanes].astype(F32)
            to_ref[:, which * 256 : (which + 1) * 256] = rebuilt.astype(BF16)
    lanes = pl.ds(pl.multiple_of(core * 512, 512), 512)
    rebuilt = ob_ref[:, lanes].astype(F32) + step_alpha * od_ref[:, lanes].astype(F32)
    rest_ref[:, 768:] = rebuilt.astype(BF16)


def lanes_of_first(rows):
    return lax.broadcasted_iota(jnp.int32, (rows, PAIR), 1) < HEAD_DIM


def split_values(v, lanes):
    nothing = jnp.zeros_like(v)
    return jnp.concatenate(
        [jnp.where(lanes, v, nothing), jnp.where(lanes, jnp.ones_like(v), nothing)], 1
    )


def causal_weights(q, k, mask):
    scores = lax.dot_general(q, k, (((1,), (1,)), ((), ())), preferred_element_type=F32)
    before = scores.shape[1] - mask.shape[1]
    last = scores[:, before:] + mask
    scores = jnp.concatenate([scores[:, :before], last], 1) if before else last
    peak = jnp.max(scores, axis=-1, keepdims=True)
    return jnp.exp2((scores - peak) * LOG2_SCALE).astype(BF16)


def block_scores(q, k):
    first = lanes_of_first(q.shape[0])
    nothing = jnp.zeros_like(q)
    keys = jnp.concatenate([jnp.where(first, k, nothing), jnp.where(first, nothing, k)], 0)
    return lax.dot_general(q, keys, (((1,), (1,)), ((), ())), preferred_element_type=F32)


def block_weights(scores, mask):
    weights = []
    for head in range(2):
        own = scores[:, head * 128 : (head + 1) * 128] + mask
        peak = jnp.max(own, axis=-1, keepdims=True)
        weights.append(jnp.exp2((own - peak) * LOG2_SCALE).astype(BF16))
    return jnp.concatenate(weights, 1)


def block_average(weights, v):
    first = lanes_of_first(v.shape[0])
    values = [split_values(v, first), split_values(v, jnp.logical_not(first))]
    both = jnp.dot(weights, jnp.concatenate(values, 0), preferred_element_type=F32)
    return (both[:, :PAIR] / both[:, PAIR:]).astype(BF16)


def row_kernel(x_hbm, *refs):
    o_hbm, x, w, normed, qkv, attended, mask_ref, sems, sems_x, sems_o = refs[8:]
    block = 256
    count = STRIDE // block
    arrive = []
    for i in range(count):
        at = pl.ds(i * block, block)
        arrive.append(pltpu.make_async_copy(x_hbm.at[at, :], x.at[at, :], sems_x.at[i]))
        arrive[i].start()
    copies = fetch_weights(refs[:8], w, sems)
    row = lax.broadcasted_iota(jnp.int32, (block, block), 0)
    col = lax.broadcasted_iota(jnp.int32, (block, block), 1)
    mask_ref[...] = jnp.where(col <= row, 0.0, -jnp.inf)
    for i in range(count):
        arrive[i].wait()
        at = slice(i * block, (i + 1) * block)
        normed[at, :] = normalized(x[at, :].astype(F32))
    for copy in copies:
        copy.wait()
    for i in range(count):
        at = slice(i * block, (i + 1) * block)
        for half in range(2):
            made = jnp.dot(normed[at, :], w[half], preferred_element_type=F32).astype(BF16)
            for which in range(3):
                for p in range(2):
                    lane = which * 256 + p * PAIR
                    qkv[which, half * 2 + p, at, :] = made[:, lane : lane + PAIR]
    leave = []
    for p in range(4):
        first = lanes_of_first(STRIDE)
        values = [split_values(qkv[2, p], first), split_values(qkv[2, p], jnp.logical_not(first))]
        shares = []
        for i in range(count):
            q, k = qkv[0, p, i * block : (i + 1) * block, :], qkv[1, p, : (i + 1) * block, :]
            mine = lanes_of_first(block)
            nothing = jnp.zeros_like(q)
            shares.append(
                [
                    causal_weights(masked, k, mask_ref[...])
                    for masked in (jnp.where(mine, q, nothing), jnp.where(mine, nothing, q))
                ]
            )
        for i in range(count):
            both = jnp.dot(
                jnp.concatenate(shares[i], 1),
                jnp.concatenate([value[: (i + 1) * block] for value in values], 0),
                preferred_element_type=F32,
            )
            attended[p, i * block : (i + 1) * block, :] = (both[:, :PAIR] / both[:, PAIR:]).astype(BF16)
        leave.append(
            pltpu.make_async_copy(attended.at[p], o_hbm.at[:, pl.ds(p * PAIR, PAIR)], sems_o.at[p])
        )
        leave[p].start()
    for copy in leave:
        copy.wait()


def sequence_row(place):
    z = ((place >> 2) & 1) * 4 + ((place >> 3) & 1) * 2 + (place >> 4)
    return ((place >> 1) & 1) * 16 + z * 2 + (place & 1)


def place_of(row):
    z = ((row >> 1) & 1) * 4 + ((row >> 2) & 1) * 2 + ((row >> 3) & 1)
    return z * 4 + (row >> 4) * 2 + (row & 1)


WIDE = 16
STEP = 32 * WIDE


def one_hot(ref, lane_of):
    wanted = lane_of(lax.broadcasted_iota(jnp.int32, (STEP, 128), 0))
    lane = lax.broadcasted_iota(jnp.int32, (STEP, 128), 1)
    for at in range(0, STEP, 128):
        ref[:, at : at + 128] = jnp.where(wanted == lane + at, 1.0, 0.0).astype(BF16)


def col_kernel(x_hbm, *refs):
    o_hbm, x, w, out, mask_ref, sort_ref, back_ref, normed_ref, sems, sems_x, sems_o = refs[8:]
    steps = x.shape[1] // WIDE
    arrive, leave = [], []
    for i in range(steps):
        at = pl.ds(i * WIDE, WIDE)
        arrive.append(pltpu.make_async_copy(x_hbm.at[:, at, :], x.at[:, at, :], sems_x.at[i]))
        leave.append(pltpu.make_async_copy(out.at[:, at, :], o_hbm.at[:, at, :], sems_o.at[i]))
        arrive[i].start()
    weights = fetch_weights(refs[:8], w, sems)
    at = lax.broadcasted_iota(jnp.int32, (128, 128), 0)
    to = lax.broadcasted_iota(jnp.int32, (128, 128), 1)
    meets = jnp.logical_and(at // 32 == to // 32, to <= at)
    mask_ref[...] = jnp.where(meets, 0.0, -jnp.inf)
    one_hot(sort_ref, lambda new: place_of(new & 31) * WIDE + (new >> 5))
    one_hot(back_ref, lambda old: (old & (WIDE - 1)) * 32 + sequence_row(old >> 4))
    for i in range(steps):
        arrive[i].wait()
        taken = x[:, i * WIDE : (i + 1) * WIDE, :].reshape(STEP, D)
        for half in range(2):
            rows = slice(half * 256, half * 256 + 256)
            ordered = jnp.dot(sort_ref[rows, :], taken, preferred_element_type=F32)
            normed_ref[i * STEP + half * 256 : i * STEP + half * 256 + 256, :] = normalized(ordered)
    for copy in weights:
        copy.wait()
    for i in range(steps):
        attended = []
        for group in range(STEP // 256):
            start = i * STEP + group * 256
            parts = [
                jnp.dot(
                    normed_ref[start : start + 256, :], w[half], preferred_element_type=F32
                ).astype(BF16)
                for half in range(2)
            ]
            blocks = []
            for made in parts:
                for p in range(2):
                    for n in (0, 128):
                        blocks.append(
                            [
                                made[n : n + 128, which * 256 + p * PAIR : which * 256 + (p + 1) * PAIR]
                                for which in range(3)
                            ]
                        )
            scores = [block_scores(q, k) for q, k, _ in blocks]
            shares = [block_weights(score, mask_ref[...]) for score in scores]
            done = [block_average(share, v) for share, (_, _, v) in zip(shares, blocks)]
            attended.append(jnp.concatenate(
                [jnp.concatenate(done[n::2], 1) for n in range(2)], 0
            ))
        back = jnp.dot(
            back_ref[...], jnp.concatenate(attended, 0), preferred_element_type=F32
        ).astype(BF16)
        out[:, i * WIDE : (i + 1) * WIDE, :] = back.reshape(32, WIDE, HALF)
        leave[i].start()
    for copy in leave:
        copy.wait()


def out_kernel(row_hbm, col_hbm, *refs):
    o_hbm, row, col, w, out, sems, sems_r, sems_c, sems_o = refs[8:]
    block = 256
    weights = fetch_weights(refs[:8], w, sems)
    rows, cols, outs = [], [], []
    for i in range(STRIDE // block):
        at = pl.ds(i * block, block)
        rows.append(pltpu.make_async_copy(row_hbm.at[at, :], row.at[at, :], sems_r.at[i]))
        cols.append(pltpu.make_async_copy(col_hbm.at[at, :], col.at[at, :], sems_c.at[i]))
        outs.append(pltpu.make_async_copy(out.at[at, :], o_hbm.at[at, :], sems_o.at[i]))
        rows[i].start()
        cols[i].start()
    for copy in weights:
        copy.wait()
    for i in range(STRIDE // block):
        at = slice(i * block, (i + 1) * block)
        rows[i].wait()
        cols[i].wait()
        for half in range(2):
            total = jnp.dot(row[at, :], w[half, :HALF, :], preferred_element_type=F32)
            total += jnp.dot(col[at, :], w[half, HALF:, :], preferred_element_type=F32)
            out[at, half * 512 : (half + 1) * 512] = total.astype(BF16)
        outs[i].start()
    for copy in outs:
        copy.wait()


ANY = pl.BlockSpec(memory_space=pl.ANY)
WHOLE = pl.BlockSpec(memory_space=pltpu.VMEM)
FAR = pl.BlockSpec(memory_space=pltpu.HBM)
DMA = pltpu.SemaphoreType.DMA


def limit(mib):
    return pltpu.CompilerParams(vmem_limit_bytes=mib << 20)


def rebuilt_half(alpha_index, *parts):
    return pl.pallas_call(
        prep_kernel,
        out_shape=[
            jax.ShapeDtypeStruct((parts[0].shape[0], width), BF16) for width in (QKV, QKV + OUT)
        ],
        in_specs=[pl.BlockSpec(memory_space=pltpu.SMEM)] + [WHOLE] * 4,
        out_specs=[WHOLE] * 2,
        compiler_params=limit(16),
        name="rebuilt_half",
    )(alpha_index, *parts)


def row_heads(sequence, slabs):
    return pl.pallas_call(
        row_kernel,
        out_shape=jax.ShapeDtypeStruct((STRIDE, HALF), BF16),
        in_specs=[FAR] + [ANY] * 8,
        out_specs=FAR,
        scratch_shapes=[
            pltpu.VMEM((STRIDE, D), BF16),
            pltpu.VMEM((2, D, QKV), BF16),
            pltpu.VMEM((STRIDE, D), BF16),
            pltpu.VMEM((3, 4, STRIDE, PAIR), BF16),
            pltpu.VMEM((4, STRIDE, PAIR), BF16),
            pltpu.VMEM((256, 256), F32),
            DMA((16,)),
            DMA((4,)),
            DMA((4,)),
        ],
        compiler_params=limit(63),
        cost_estimate=pl.CostEstimate(
            flops=6_000_000_000, bytes_accessed=6 << 20, transcendentals=5_000_000
        ),
        name="row_heads",
    )(sequence, *slabs)


def col_heads(columns, slabs):
    rows, cols = columns.shape[:2]
    return pl.pallas_call(
        col_kernel,
        out_shape=jax.ShapeDtypeStruct((rows, cols, HALF), BF16),
        in_specs=[FAR] + [ANY] * 8,
        out_specs=FAR,
        scratch_shapes=[
            pltpu.VMEM((rows, cols, D), BF16),
            pltpu.VMEM((2, D, QKV), BF16),
            pltpu.VMEM((rows, cols, HALF), BF16),
            pltpu.VMEM((128, 128), F32),
            pltpu.VMEM((STEP, STEP), BF16),
            pltpu.VMEM((STEP, STEP), BF16),
            pltpu.VMEM((rows * cols, D), BF16),
            DMA((16,)),
            DMA((cols // WIDE,)),
            DMA((cols // WIDE,)),
        ],
        compiler_params=limit(63),
        cost_estimate=pl.CostEstimate(
            flops=4_000_000_000, bytes_accessed=6 << 20, transcendentals=1_000_000
        ),
        name="col_heads",
    )(columns, *slabs)


def project_out(row_out, col_out, slabs):
    return pl.pallas_call(
        out_kernel,
        out_shape=jax.ShapeDtypeStruct((STRIDE, D), BF16),
        in_specs=[FAR] * 2 + [ANY] * 8,
        out_specs=FAR,
        scratch_shapes=[
            pltpu.VMEM((STRIDE, HALF), BF16),
            pltpu.VMEM((STRIDE, HALF), BF16),
            pltpu.VMEM((2, D, OUT), BF16),
            pltpu.VMEM((STRIDE, D), BF16),
            DMA((16,)),
            DMA((4,)),
            DMA((4,)),
            DMA((4,)),
        ],
        compiler_params=limit(63),
        cost_estimate=pl.CostEstimate(
            flops=2_000_000_000, bytes_accessed=6 << 20, transcendentals=0
        ),
        name="project_out",
    )(row_out, col_out, *slabs)


ORDER = [sequence_row(place) for place in range(32)]


def exchange(blocks):
    return lax.all_to_all(
        blocks, "seq", split_axis=0, concat_axis=0, tiled=True, axis_index_groups=[ORDER]
    )


def with_far_y(own):
    return jnp.stack([own, send(own, hop(1, 0))])


def along_x(both):
    return [both] + [send(both, hop(0, dx)) for dx in range(1, 4)]


def both_cores(pieces):
    return pieces + [send(piece, CORE) for piece in pieces]


def shards(tokens, qkv_base, qkv_dir, out_base, out_dir, alpha_index):
    sequence = tokens[0]
    columns = exchange(sequence.reshape(32, 32, D))
    own_cols, own_rest = rebuilt_half(alpha_index, qkv_base, qkv_dir, out_base, out_dir)
    col_pieces = along_x(with_far_y(own_cols))
    rest, col_pieces = lax.optimization_barrier((with_far_y(own_rest), col_pieces))
    row_pieces = along_x(rest[:, :, :QKV])
    attended = col_heads(columns, both_cores(col_pieces))
    row_pieces, rest, attended = lax.optimization_barrier((row_pieces, rest, attended))
    col_out = exchange(attended)
    out_pieces = along_x(rest[:, :, QKV:])
    row_out = row_heads(sequence, both_cores(row_pieces))
    out_pieces, row_out = lax.optimization_barrier((out_pieces, row_out))
    return project_out(row_out, col_out.reshape(STRIDE, HALF), both_cores(out_pieces))[None]


def solution(mesh):
    in_specs = (
        P("fsdp", "seq", None),
        P("fsdp", None),
        P("fsdp", None),
        P("fsdp", None),
        P("fsdp", None),
        P(),
    )
    out_specs = P("fsdp", "seq", None)
    return jax.shard_map(shards, mesh=mesh, in_specs=in_specs, out_specs=out_specs, check_vma=False)
```

```python
import math

import jax
import jax.numpy as jnp
from jax import lax
from jax.experimental import pallas as pl
from jax.experimental.pallas import tpu as pltpu
from jax.sharding import PartitionSpec as P

D = 1024
HEADS = 16
STRIDE = 1024
NALPHA = 1024
HEAD_DIM = D // HEADS
HALF = D // 2
PAIR = 2 * HEAD_DIM
QKV, OUT = 768, 512
F32, BF16 = jnp.float32, jnp.bfloat16
LOG2_SCALE = math.log2(math.e) / math.sqrt(HEAD_DIM)
BOTH = ("seq", "fsdp")


def split_index(i):
    s, f = divmod(i, 8)
    return s // 16, (s // 2) % 8, s % 2, f // 4, f % 4


def pairs(move):
    out = []
    for i in range(256):
        yl, z, c, yh, x = move(*split_index(i))
        out.append((i, ((yl * 8 + z) * 2 + c) * 8 + yh * 4 + x))
    return out


def hop(other_y, dx):
    return pairs(
        lambda yl, z, c, yh, x: (yl ^ other_y, z, c, yh ^ other_y, (x + dx) % 4)
    )


CORE = pairs(lambda yl, z, c, yh, x: (yl, z, 1 - c, yh, x))


def send(value, where):
    return lax.ppermute(value, BOTH, where)


def normalized(rows):
    mean_square = jnp.mean(rows * rows, axis=-1, keepdims=True)
    return (rows * lax.rsqrt(mean_square + 1e-06)).astype(BF16)


def fetch_weights(slabs, dest, sems):
    core = lax.axis_index("seq") % 2
    mine = lax.axis_index("fsdp")
    copies = []
    for n, slab in enumerate(slabs):
        half = core if n < 4 else 1 - core
        for k in range(2):
            y_hi = mine // 4 if k == 0 else 1 - mine // 4
            feature = pl.multiple_of((y_hi * 4 + (mine % 4 - n % 4 + 4) % 4) * 128, 128)
            copy = pltpu.make_async_copy(
                slab.at[k],
                dest.at[half, pl.ds(feature, 128), :],
                sems.at[n * 2 + k],
            )
            copy.start()
            copies.append(copy)
    return copies


def prep_kernel(alpha_ref, qb_ref, qd_ref, ob_ref, od_ref, cols_ref, rest_ref):
    core = lax.axis_index("seq") % 2
    step_alpha = (alpha_ref[0].astype(F32) + NALPHA) / (2.0 * NALPHA)
    for kind, to_ref in ((1, cols_ref), (0, rest_ref)):
        for which in range(3):
            lanes = pl.ds(pl.multiple_of(which * D + kind * HALF + core * 256, 256), 256)
            rebuilt = qb_ref[:, lanes].astype(F32) + step_alpha * qd_ref[:, lanes].astype(F32)
            to_ref[:, which * 256 : (which + 1) * 256] = rebuilt.astype(BF16)
    lanes = pl.ds(pl.multiple_of(core * 512, 512), 512)
    rebuilt = ob_ref[:, lanes].astype(F32) + step_alpha * od_ref[:, lanes].astype(F32)
    rest_ref[:, 768:] = rebuilt.astype(BF16)


def lanes_of_first(rows):
    return lax.broadcasted_iota(jnp.int32, (rows, PAIR), 1) < HEAD_DIM


def split_values(v, lanes):
    nothing = jnp.zeros_like(v)
    return jnp.concatenate(
        [jnp.where(lanes, v, nothing), jnp.where(lanes, jnp.ones_like(v), nothing)], 1
    )


def causal_weights(q, k, mask):
    scores = lax.dot_general(q, k, (((1,), (1,)), ((), ())), preferred_element_type=F32)
    before = scores.shape[1] - mask.shape[1]
    last = scores[:, before:] + mask
    scores = jnp.concatenate([scores[:, :before], last], 1) if before else last
    peak = jnp.max(scores, axis=-1, keepdims=True)
    return jnp.exp2((scores - peak) * LOG2_SCALE).astype(BF16)


def block_scores(q, k):
    first = lanes_of_first(q.shape[0])
    nothing = jnp.zeros_like(q)
    keys = jnp.concatenate([jnp.where(first, k, nothing), jnp.where(first, nothing, k)], 0)
    return lax.dot_general(q, keys, (((1,), (1,)), ((), ())), preferred_element_type=F32)


def block_weights(scores, mask):
    weights = []
    for head in range(2):
        own = scores[:, head * 128 : (head + 1) * 128] + mask
        peak = jnp.max(own, axis=-1, keepdims=True)
        weights.append(jnp.exp2((own - peak) * LOG2_SCALE).astype(BF16))
    return jnp.concatenate(weights, 1)


def block_average(weights, v):
    first = lanes_of_first(v.shape[0])
    values = [split_values(v, first), split_values(v, jnp.logical_not(first))]
    both = jnp.dot(weights, jnp.concatenate(values, 0), preferred_element_type=F32)
    return (both[:, :PAIR] / both[:, PAIR:]).astype(BF16)


def row_kernel(x_hbm, *refs):
    o_hbm, x, w, normed, qkv, attended, mask_ref, sems, sems_x, sems_o = refs[8:]
    block = 256
    count = STRIDE // block
    arrive = []
    for i in range(count):
        at = pl.ds(i * block, block)
        arrive.append(pltpu.make_async_copy(x_hbm.at[at, :], x.at[at, :], sems_x.at[i]))
        arrive[i].start()
    copies = fetch_weights(refs[:8], w, sems)
    row = lax.broadcasted_iota(jnp.int32, (block, block), 0)
    col = lax.broadcasted_iota(jnp.int32, (block, block), 1)
    mask_ref[...] = jnp.where(col <= row, 0.0, -jnp.inf)
    for i in range(count):
        arrive[i].wait()
        at = slice(i * block, (i + 1) * block)
        normed[at, :] = normalized(x[at, :].astype(F32))
    for copy in copies:
        copy.wait()
    for i in range(count):
        at = slice(i * block, (i + 1) * block)
        for half in range(2):
            made = jnp.dot(normed[at, :], w[half], preferred_element_type=F32).astype(BF16)
            for which in range(3):
                for p in range(2):
                    lane = which * 256 + p * PAIR
                    qkv[which, half * 2 + p, at, :] = made[:, lane : lane + PAIR]
    leave = []
    for p in range(4):
        first = lanes_of_first(STRIDE)
        values = [split_values(qkv[2, p], first), split_values(qkv[2, p], jnp.logical_not(first))]
        shares = []
        for i in range(count):
            q, k = qkv[0, p, i * block : (i + 1) * block, :], qkv[1, p, : (i + 1) * block, :]
            mine = lanes_of_first(block)
            nothing = jnp.zeros_like(q)
            shares.append(
                [
                    causal_weights(masked, k, mask_ref[...])
                    for masked in (jnp.where(mine, q, nothing), jnp.where(mine, nothing, q))
                ]
            )
        for i in range(count):
            both = jnp.dot(
                jnp.concatenate(shares[i], 1),
                jnp.concatenate([value[: (i + 1) * block] for value in values], 0),
                preferred_element_type=F32,
            )
            attended[p, i * block : (i + 1) * block, :] = (both[:, :PAIR] / both[:, PAIR:]).astype(BF16)
        leave.append(
            pltpu.make_async_copy(attended.at[p], o_hbm.at[:, pl.ds(p * PAIR, PAIR)], sems_o.at[p])
        )
        leave[p].start()
    for copy in leave:
        copy.wait()


def sequence_row(place):
    z = ((place >> 2) & 1) * 4 + ((place >> 3) & 1) * 2 + (place >> 4)
    return ((place >> 1) & 1) * 16 + z * 2 + (place & 1)


def place_of(row):
    z = ((row >> 1) & 1) * 4 + ((row >> 2) & 1) * 2 + ((row >> 3) & 1)
    return z * 4 + (row >> 4) * 2 + (row & 1)


WIDE = 16
STEP = 32 * WIDE


def one_hot(ref, lane_of):
    wanted = lane_of(lax.broadcasted_iota(jnp.int32, (STEP, 128), 0))
    lane = lax.broadcasted_iota(jnp.int32, (STEP, 128), 1)
    for at in range(0, STEP, 128):
        ref[:, at : at + 128] = jnp.where(wanted == lane + at, 1.0, 0.0).astype(BF16)


def col_kernel(x_hbm, *refs):
    o_hbm, x, w, out, mask_ref, sort_ref, back_ref, normed_ref, sems, sems_x, sems_o = refs[8:]
    steps = x.shape[1] // WIDE
    arrive, leave = [], []
    for i in range(steps):
        at = pl.ds(i * WIDE, WIDE)
        arrive.append(pltpu.make_async_copy(x_hbm.at[:, at, :], x.at[:, at, :], sems_x.at[i]))
        leave.append(pltpu.make_async_copy(out.at[:, at, :], o_hbm.at[:, at, :], sems_o.at[i]))
        arrive[i].start()
    weights = fetch_weights(refs[:8], w, sems)
    at = lax.broadcasted_iota(jnp.int32, (128, 128), 0)
    to = lax.broadcasted_iota(jnp.int32, (128, 128), 1)
    meets = jnp.logical_and(at // 32 == to // 32, to <= at)
    mask_ref[...] = jnp.where(meets, 0.0, -jnp.inf)
    one_hot(sort_ref, lambda new: place_of(new & 31) * WIDE + (new >> 5))
    one_hot(back_ref, lambda old: (old & (WIDE - 1)) * 32 + sequence_row(old >> 4))
    for i in range(steps):
        arrive[i].wait()
        taken = x[:, i * WIDE : (i + 1) * WIDE, :].reshape(STEP, D)
        for half in range(2):
            rows = slice(half * 256, half * 256 + 256)
            ordered = jnp.dot(sort_ref[rows, :], taken, preferred_element_type=F32)
            normed_ref[i * STEP + half * 256 : i * STEP + half * 256 + 256, :] = normalized(ordered)
    for copy in weights:
        copy.wait()
    for i in range(steps):
        attended = []
        for group in range(STEP // 256):
            start = i * STEP + group * 256
            parts = [
                jnp.dot(
                    normed_ref[start : start + 256, :], w[half], preferred_element_type=F32
                ).astype(BF16)
                for half in range(2)
            ]
            blocks = []
            for made in parts:
                for p in range(2):
                    for n in (0, 128):
                        blocks.append(
                            [
                                made[n : n + 128, which * 256 + p * PAIR : which * 256 + (p + 1) * PAIR]
                                for which in range(3)
                            ]
                        )
            scores = [block_scores(q, k) for q, k, _ in blocks]
            shares = [block_weights(score, mask_ref[...]) for score in scores]
            done = [block_average(share, v) for share, (_, _, v) in zip(shares, blocks)]
            attended.append(jnp.concatenate(
                [jnp.concatenate(done[n::2], 1) for n in range(2)], 0
            ))
        back = jnp.dot(
            back_ref[...], jnp.concatenate(attended, 0), preferred_element_type=F32
        ).astype(BF16)
        out[:, i * WIDE : (i + 1) * WIDE, :] = back.reshape(32, WIDE, HALF)
        leave[i].start()
    for copy in leave:
        copy.wait()


def out_kernel(row, col, *refs):
    o_hbm, w, out, sems, sems_o = refs[8:]
    block = 256
    outs = []
    for copy in fetch_weights(refs[:8], w, sems):
        copy.wait()
    for i in range(STRIDE // block):
        at = slice(i * block, (i + 1) * block)
        for half in range(2):
            total = jnp.dot(row[at, :], w[half, :HALF, :], preferred_element_type=F32)
            total += jnp.dot(col[at, :], w[half, HALF:, :], preferred_element_type=F32)
            out[at, half * 512 : (half + 1) * 512] = total.astype(BF16)
        outs.append(pltpu.make_async_copy(out.at[at, :], o_hbm.at[at, :], sems_o.at[i]))
        outs[i].start()
    for copy in outs:
        copy.wait()


ANY = pl.BlockSpec(memory_space=pl.ANY)
WHOLE = pl.BlockSpec(memory_space=pltpu.VMEM)
FAR = pl.BlockSpec(memory_space=pltpu.HBM)
DMA = pltpu.SemaphoreType.DMA


def limit(mib):
    return pltpu.CompilerParams(vmem_limit_bytes=mib << 20)


def rebuilt_half(alpha_index, *parts):
    return pl.pallas_call(
        prep_kernel,
        out_shape=[
            jax.ShapeDtypeStruct((parts[0].shape[0], width), BF16) for width in (QKV, QKV + OUT)
        ],
        in_specs=[pl.BlockSpec(memory_space=pltpu.SMEM)] + [WHOLE] * 4,
        out_specs=[WHOLE] * 2,
        compiler_params=limit(16),
        name="rebuilt_half",
    )(alpha_index, *parts)


def row_heads(sequence, slabs):
    return pl.pallas_call(
        row_kernel,
        out_shape=jax.ShapeDtypeStruct((STRIDE, HALF), BF16),
        in_specs=[FAR] + [ANY] * 8,
        out_specs=ANY,
        scratch_shapes=[
            pltpu.VMEM((STRIDE, D), BF16),
            pltpu.VMEM((2, D, QKV), BF16),
            pltpu.VMEM((STRIDE, D), BF16),
            pltpu.VMEM((3, 4, STRIDE, PAIR), BF16),
            pltpu.VMEM((4, STRIDE, PAIR), BF16),
            pltpu.VMEM((256, 256), F32),
            DMA((16,)),
            DMA((4,)),
            DMA((4,)),
        ],
        compiler_params=limit(48),
        cost_estimate=pl.CostEstimate(
            flops=6_000_000_000, bytes_accessed=6 << 20, transcendentals=5_000_000
        ),
        name="row_heads",
    )(sequence, *slabs)


def col_heads(columns, slabs):
    rows, cols = columns.shape[:2]
    return pl.pallas_call(
        col_kernel,
        out_shape=jax.ShapeDtypeStruct((rows, cols, HALF), BF16),
        in_specs=[FAR] + [ANY] * 8,
        out_specs=FAR,
        scratch_shapes=[
            pltpu.VMEM((rows, cols, D), BF16),
            pltpu.VMEM((2, D, QKV), BF16),
            pltpu.VMEM((rows, cols, HALF), BF16),
            pltpu.VMEM((128, 128), F32),
            pltpu.VMEM((STEP, STEP), BF16),
            pltpu.VMEM((STEP, STEP), BF16),
            pltpu.VMEM((rows * cols, D), BF16),
            DMA((16,)),
            DMA((cols // WIDE,)),
            DMA((cols // WIDE,)),
        ],
        compiler_params=limit(63),
        cost_estimate=pl.CostEstimate(
            flops=4_000_000_000, bytes_accessed=6 << 20, transcendentals=1_000_000
        ),
        name="col_heads",
    )(columns, *slabs)


def project_out(row_out, col_out, slabs):
    return pl.pallas_call(
        out_kernel,
        out_shape=jax.ShapeDtypeStruct((STRIDE, D), BF16),
        in_specs=[WHOLE] * 2 + [ANY] * 8,
        out_specs=FAR,
        scratch_shapes=[
            pltpu.VMEM((2, D, OUT), BF16),
            pltpu.VMEM((STRIDE, D), BF16),
            DMA((16,)),
            DMA((4,)),
        ],
        compiler_params=limit(24),
        cost_estimate=pl.CostEstimate(
            flops=2_000_000_000, bytes_accessed=6 << 20, transcendentals=0
        ),
        name="project_out",
    )(row_out, col_out, *slabs)


ORDER = [sequence_row(place) for place in range(32)]


def exchange(blocks):
    return lax.all_to_all(
        blocks, "seq", split_axis=0, concat_axis=0, tiled=True, axis_index_groups=[ORDER]
    )


def with_far_y(own):
    return jnp.stack([own, send(own, hop(1, 0))])


def along_x(both):
    return [both] + [send(both, hop(0, dx)) for dx in range(1, 4)]


def both_cores(pieces):
    return pieces + [send(piece, CORE) for piece in pieces]


def shards(tokens, qkv_base, qkv_dir, out_base, out_dir, alpha_index):
    sequence = tokens[0]
    columns = exchange(sequence.reshape(32, 32, D))
    own_cols, own_rest = rebuilt_half(alpha_index, qkv_base, qkv_dir, out_base, out_dir)
    col_pieces = along_x(with_far_y(own_cols))
    rest, col_pieces = lax.optimization_barrier((with_far_y(own_rest), col_pieces))
    row_pieces = along_x(rest[:, :, :QKV])
    attended = col_heads(columns, both_cores(col_pieces))
    row_pieces, rest, attended = lax.optimization_barrier((row_pieces, rest, attended))
    col_out = exchange(attended)
    out_pieces = along_x(rest[:, :, QKV:])
    row_out = row_heads(sequence, both_cores(row_pieces))
    out_pieces, row_out = lax.optimization_barrier((out_pieces, row_out))
    return project_out(row_out, col_out.reshape(STRIDE, HALF), both_cores(out_pieces))[None]


def solution(mesh):
    in_specs = (
        P("fsdp", "seq", None),
        P("fsdp", None),
        P("fsdp", None),
        P("fsdp", None),
        P("fsdp", None),
        P(),
    )
    out_specs = P("fsdp", "seq", None)
    return jax.shard_map(shards, mesh=mesh, in_specs=in_specs, out_specs=out_specs, check_vma=False)
```

```python
import math

import jax
import jax.numpy as jnp
from jax import lax
from jax.experimental import pallas as pl
from jax.experimental.pallas import tpu as pltpu
from jax.sharding import PartitionSpec as P

D = 1024
HEADS = 16
STRIDE = 1024
NALPHA = 1024
HEAD_DIM = D // HEADS
HALF = D // 2
PAIR = 2 * HEAD_DIM
QKV, OUT = 768, 512
F32, BF16 = jnp.float32, jnp.bfloat16
LOG2_SCALE = math.log2(math.e) / math.sqrt(HEAD_DIM)
BOTH = ("seq", "fsdp")


def split_index(i):
    s, f = divmod(i, 8)
    return s // 16, (s // 2) % 8, s % 2, f // 4, f % 4


def pairs(move):
    out = []
    for i in range(256):
        yl, z, c, yh, x = move(*split_index(i))
        out.append((i, ((yl * 8 + z) * 2 + c) * 8 + yh * 4 + x))
    return out


def hop(other_y, dx):
    return pairs(
        lambda yl, z, c, yh, x: (yl ^ other_y, z, c, yh ^ other_y, (x + dx) % 4)
    )


CORE = pairs(lambda yl, z, c, yh, x: (yl, z, 1 - c, yh, x))


def send(value, where):
    return lax.ppermute(value, BOTH, where)


def normalized(rows):
    mean_square = jnp.mean(rows * rows, axis=-1, keepdims=True)
    return (rows * lax.rsqrt(mean_square + 1e-06)).astype(BF16)


def fetch_weights(slabs, dest, sems):
    core = lax.axis_index("seq") % 2
    mine = lax.axis_index("fsdp")
    copies = []
    for n, slab in enumerate(slabs):
        half = core if n < 4 else 1 - core
        for k in range(2):
            y_hi = mine // 4 if k == 0 else 1 - mine // 4
            feature = pl.multiple_of((y_hi * 4 + (mine % 4 - n % 4 + 4) % 4) * 128, 128)
            copy = pltpu.make_async_copy(
                slab.at[k],
                dest.at[half, pl.ds(feature, 128), :],
                sems.at[n * 2 + k],
            )
            copy.start()
            copies.append(copy)
    return copies


def prep_kernel(alpha_ref, qb_ref, qd_ref, ob_ref, od_ref, cols_ref, rest_ref):
    core = lax.axis_index("seq") % 2
    step_alpha = (alpha_ref[0].astype(F32) + NALPHA) / (2.0 * NALPHA)
    for kind, to_ref in ((1, cols_ref), (0, rest_ref)):
        for which in range(3):
            lanes = pl.ds(pl.multiple_of(which * D + kind * HALF + core * 256, 256), 256)
            rebuilt = qb_ref[:, lanes].astype(F32) + step_alpha * qd_ref[:, lanes].astype(F32)
            to_ref[:, which * 256 : (which + 1) * 256] = rebuilt.astype(BF16)
    lanes = pl.ds(pl.multiple_of(core * 512, 512), 512)
    rebuilt = ob_ref[:, lanes].astype(F32) + step_alpha * od_ref[:, lanes].astype(F32)
    rest_ref[:, 768:] = rebuilt.astype(BF16)


def lanes_of_first(rows):
    return lax.broadcasted_iota(jnp.int32, (rows, PAIR), 1) < HEAD_DIM


def split_values(v, lanes):
    nothing = jnp.zeros_like(v)
    return jnp.concatenate(
        [jnp.where(lanes, v, nothing), jnp.where(lanes, jnp.ones_like(v), nothing)], 1
    )


def causal_weights(q, k, mask):
    scores = lax.dot_general(q, k, (((1,), (1,)), ((), ())), preferred_element_type=F32)
    before = scores.shape[1] - mask.shape[1]
    last = scores[:, before:] + mask
    scores = jnp.concatenate([scores[:, :before], last], 1) if before else last
    peak = jnp.max(scores, axis=-1, keepdims=True)
    return jnp.exp2((scores - peak) * LOG2_SCALE).astype(BF16)


def block_scores(q, k):
    first = lanes_of_first(q.shape[0])
    nothing = jnp.zeros_like(q)
    keys = jnp.concatenate([jnp.where(first, k, nothing), jnp.where(first, nothing, k)], 0)
    return lax.dot_general(q, keys, (((1,), (1,)), ((), ())), preferred_element_type=F32)


def block_weights(scores, mask):
    weights = []
    for head in range(2):
        own = scores[:, head * 128 : (head + 1) * 128] + mask
        peak = jnp.max(own, axis=-1, keepdims=True)
        weights.append(jnp.exp2((own - peak) * LOG2_SCALE).astype(BF16))
    return jnp.concatenate(weights, 1)


def block_average(weights, v):
    first = lanes_of_first(v.shape[0])
    values = [split_values(v, first), split_values(v, jnp.logical_not(first))]
    both = jnp.dot(weights, jnp.concatenate(values, 0), preferred_element_type=F32)
    return (both[:, :PAIR] / both[:, PAIR:]).astype(BF16)


def row_kernel(x_hbm, *refs):
    o_hbm, x, w, normed, qkv, attended, mask_ref, sems, sems_x, sems_o = refs[8:]
    block = 256
    count = STRIDE // block
    arrive = []
    for i in range(count):
        at = pl.ds(i * block, block)
        arrive.append(pltpu.make_async_copy(x_hbm.at[at, :], x.at[at, :], sems_x.at[i]))
        arrive[i].start()
    copies = fetch_weights(refs[:8], w, sems)
    row = lax.broadcasted_iota(jnp.int32, (block, block), 0)
    col = lax.broadcasted_iota(jnp.int32, (block, block), 1)
    mask_ref[...] = jnp.where(col <= row, 0.0, -jnp.inf)
    for i in range(count):
        arrive[i].wait()
        at = slice(i * block, (i + 1) * block)
        normed[at, :] = normalized(x[at, :].astype(F32))
    for copy in copies:
        copy.wait()
    for i in range(count):
        at = slice(i * block, (i + 1) * block)
        for half in range(2):
            made = jnp.dot(normed[at, :], w[half], preferred_element_type=F32).astype(BF16)
            for which in range(3):
                for p in range(2):
                    lane = which * 256 + p * PAIR
                    qkv[which, half * 2 + p, at, :] = made[:, lane : lane + PAIR]
    leave = []
    for p in range(4):
        first = lanes_of_first(STRIDE)
        values = [split_values(qkv[2, p], first), split_values(qkv[2, p], jnp.logical_not(first))]
        shares = []
        for i in range(count):
            q, k = qkv[0, p, i * block : (i + 1) * block, :], qkv[1, p, : (i + 1) * block, :]
            mine = lanes_of_first(block)
            nothing = jnp.zeros_like(q)
            shares.append(
                [
                    causal_weights(masked, k, mask_ref[...])
                    for masked in (jnp.where(mine, q, nothing), jnp.where(mine, nothing, q))
                ]
            )
        for i in range(count):
            both = jnp.dot(
                jnp.concatenate(shares[i], 1),
                jnp.concatenate([value[: (i + 1) * block] for value in values], 0),
                preferred_element_type=F32,
            )
            attended[p, i * block : (i + 1) * block, :] = (both[:, :PAIR] / both[:, PAIR:]).astype(BF16)
        leave.append(
            pltpu.make_async_copy(attended.at[p], o_hbm.at[:, pl.ds(p * PAIR, PAIR)], sems_o.at[p])
        )
        leave[p].start()
    for copy in leave:
        copy.wait()


def sequence_row(place):
    z = ((place >> 2) & 1) * 4 + ((place >> 3) & 1) * 2 + (place >> 4)
    return ((place >> 1) & 1) * 16 + z * 2 + (place & 1)


CHUNK = 16
TILE = CHUNK * CHUNK


def col_kernel(x_hbm, *refs):
    o_hbm, x, w, out, mask_ref, turn_ref, normed_ref, sems, sems_x, sems_o = refs[8:]
    steps = x.shape[1] // CHUNK
    arrive, leave = [], []
    for i in range(steps):
        at = pl.ds(i * CHUNK, CHUNK)
        arrive.append(pltpu.make_async_copy(x_hbm.at[:, at, :], x.at[:, at, :], sems_x.at[i]))
        leave.append(pltpu.make_async_copy(out.at[:, at, :], o_hbm.at[:, at, :], sems_o.at[i]))
        arrive[i].start()
    weights = fetch_weights(refs[:8], w, sems)
    at = lax.broadcasted_iota(jnp.int32, (128, 128), 0)
    to = lax.broadcasted_iota(jnp.int32, (128, 128), 1)
    query_row = sequence_row((at >> 6) * CHUNK + (at & 15))
    key_row = sequence_row((to >> 6) * CHUNK + (to & 15))
    meets = jnp.logical_and(((at ^ to) & 48) == 0, key_row <= query_row)
    mask_ref[...] = jnp.where(meets, 0.0, -jnp.inf)
    new = lax.broadcasted_iota(jnp.int32, (TILE, TILE), 0)
    old = lax.broadcasted_iota(jnp.int32, (TILE, TILE), 1)
    turn_ref[...] = jnp.where(new == (old & 15) * CHUNK + (old >> 4), 1.0, 0.0).astype(BF16)
    for i in range(steps):
        arrive[i].wait()
        for half in range(2):
            taken = x[half * CHUNK : (half + 1) * CHUNK, i * CHUNK : (i + 1) * CHUNK, :]
            ordered = jnp.dot(
                turn_ref[...], taken.reshape(TILE, D), preferred_element_type=F32
            )
            normed = normalized(ordered)
            for block in range(4):
                start = i * 2 * TILE + block * 128 + half * 64
                normed_ref[start : start + 64, :] = normed[block * 64 : (block + 1) * 64, :]
    for copy in weights:
        copy.wait()
    for i in range(steps):
        attended = []
        for group in range(2):
            start = (i * 2 + group) * TILE
            parts = [
                jnp.dot(
                    normed_ref[start : start + TILE, :], w[half], preferred_element_type=F32
                ).astype(BF16)
                for half in range(2)
            ]
            blocks = []
            for made in parts:
                for p in range(2):
                    for n in (0, 128):
                        blocks.append(
                            [
                                made[n : n + 128, which * 256 + p * PAIR : which * 256 + (p + 1) * PAIR]
                                for which in range(3)
                            ]
                        )
            scores = [block_scores(q, k) for q, k, _ in blocks]
            shares = [block_weights(score, mask_ref[...]) for score in scores]
            done = [block_average(share, v) for share, (_, _, v) in zip(shares, blocks)]
            attended += [jnp.concatenate(done[n::2], 1) for n in range(2)]
        for half in range(2):
            back = jnp.dot(
                turn_ref[...],
                jnp.concatenate([block[half * 64 : half * 64 + 64] for block in attended], 0),
                preferred_element_type=F32,
            ).astype(BF16)
            out[half * CHUNK : (half + 1) * CHUNK, i * CHUNK : (i + 1) * CHUNK, :] = back.reshape(
                CHUNK, CHUNK, HALF
            )
        leave[i].start()
    for copy in leave:
        copy.wait()


def out_kernel(row_hbm, col_hbm, *refs):
    o_hbm, row, col, w, out, sems, sems_r, sems_c, sems_o = refs[8:]
    block = 256
    weights = fetch_weights(refs[:8], w, sems)
    rows, cols, outs = [], [], []
    for i in range(STRIDE // block):
        at = pl.ds(i * block, block)
        rows.append(pltpu.make_async_copy(row_hbm.at[at, :], row.at[at, :], sems_r.at[i]))
        cols.append(pltpu.make_async_copy(col_hbm.at[at, :], col.at[at, :], sems_c.at[i]))
        outs.append(pltpu.make_async_copy(out.at[at, :], o_hbm.at[at, :], sems_o.at[i]))
        rows[i].start()
        cols[i].start()
    for copy in weights:
        copy.wait()
    for i in range(STRIDE // block):
        at = slice(i * block, (i + 1) * block)
        rows[i].wait()
        cols[i].wait()
        for half in range(2):
            total = jnp.dot(row[at, :], w[half, :HALF, :], preferred_element_type=F32)
            total += jnp.dot(col[at, :], w[half, HALF:, :], preferred_element_type=F32)
            out[at, half * 512 : (half + 1) * 512] = total.astype(BF16)
        outs[i].start()
    for copy in outs:
        copy.wait()


ANY = pl.BlockSpec(memory_space=pl.ANY)
WHOLE = pl.BlockSpec(memory_space=pltpu.VMEM)
FAR = pl.BlockSpec(memory_space=pltpu.HBM)
DMA = pltpu.SemaphoreType.DMA


def limit(mib):
    return pltpu.CompilerParams(vmem_limit_bytes=mib << 20)


def rebuilt_half(alpha_index, *parts):
    return pl.pallas_call(
        prep_kernel,
        out_shape=[
            jax.ShapeDtypeStruct((parts[0].shape[0], width), BF16) for width in (QKV, QKV + OUT)
        ],
        in_specs=[pl.BlockSpec(memory_space=pltpu.SMEM)] + [WHOLE] * 4,
        out_specs=[WHOLE] * 2,
        compiler_params=limit(16),
        name="rebuilt_half",
    )(alpha_index, *parts)


def row_heads(sequence, slabs):
    return pl.pallas_call(
        row_kernel,
        out_shape=jax.ShapeDtypeStruct((STRIDE, HALF), BF16),
        in_specs=[FAR] + [ANY] * 8,
        out_specs=FAR,
        scratch_shapes=[
            pltpu.VMEM((STRIDE, D), BF16),
            pltpu.VMEM((2, D, QKV), BF16),
            pltpu.VMEM((STRIDE, D), BF16),
            pltpu.VMEM((3, 4, STRIDE, PAIR), BF16),
            pltpu.VMEM((4, STRIDE, PAIR), BF16),
            pltpu.VMEM((256, 256), F32),
            DMA((16,)),
            DMA((4,)),
            DMA((4,)),
        ],
        compiler_params=limit(63),
        cost_estimate=pl.CostEstimate(
            flops=6_000_000_000, bytes_accessed=6 << 20, transcendentals=5_000_000
        ),
        name="row_heads",
    )(sequence, *slabs)


def col_heads(columns, slabs):
    rows, cols = columns.shape[:2]
    return pl.pallas_call(
        col_kernel,
        out_shape=jax.ShapeDtypeStruct((rows, cols, HALF), BF16),
        in_specs=[FAR] + [ANY] * 8,
        out_specs=FAR,
        scratch_shapes=[
            pltpu.VMEM((rows, cols, D), BF16),
            pltpu.VMEM((2, D, QKV), BF16),
            pltpu.VMEM((rows, cols, HALF), BF16),
            pltpu.VMEM((128, 128), F32),
            pltpu.VMEM((TILE, TILE), BF16),
            pltpu.VMEM((rows * cols, D), BF16),
            DMA((16,)),
            DMA((cols // CHUNK,)),
            DMA((cols // CHUNK,)),
        ],
        compiler_params=limit(63),
        cost_estimate=pl.CostEstimate(
            flops=4_000_000_000, bytes_accessed=6 << 20, transcendentals=1_000_000
        ),
        name="col_heads",
    )(columns, *slabs)


def project_out(row_out, col_out, slabs):
    return pl.pallas_call(
        out_kernel,
        out_shape=jax.ShapeDtypeStruct((STRIDE, D), BF16),
        in_specs=[FAR] * 2 + [ANY] * 8,
        out_specs=FAR,
        scratch_shapes=[
            pltpu.VMEM((STRIDE, HALF), BF16),
            pltpu.VMEM((STRIDE, HALF), BF16),
            pltpu.VMEM((2, D, OUT), BF16),
            pltpu.VMEM((STRIDE, D), BF16),
            DMA((16,)),
            DMA((4,)),
            DMA((4,)),
            DMA((4,)),
        ],
        compiler_params=limit(63),
        cost_estimate=pl.CostEstimate(
            flops=2_000_000_000, bytes_accessed=6 << 20, transcendentals=0
        ),
        name="project_out",
    )(row_out, col_out, *slabs)


ORDER = [sequence_row(place) for place in range(32)]


def exchange(blocks):
    return lax.all_to_all(
        blocks, "seq", split_axis=0, concat_axis=0, tiled=True, axis_index_groups=[ORDER]
    )


def with_far_y(own):
    return jnp.stack([own, send(own, hop(1, 0))])


def along_x(both):
    return [both] + [send(both, hop(0, dx)) for dx in range(1, 4)]


def both_cores(pieces):
    return pieces + [send(piece, CORE) for piece in pieces]


def shards(tokens, qkv_base, qkv_dir, out_base, out_dir, alpha_index):
    sequence = tokens[0]
    columns = exchange(sequence.reshape(32, 32, D))
    own_cols, own_rest = rebuilt_half(alpha_index, qkv_base, qkv_dir, out_base, out_dir)
    col_pieces = along_x(with_far_y(own_cols))
    rest, col_pieces = lax.optimization_barrier((with_far_y(own_rest), col_pieces))
    row_pieces = along_x(rest[:, :, :QKV])
    attended = col_heads(columns, both_cores(col_pieces))
    row_pieces, rest, attended = lax.optimization_barrier((row_pieces, rest, attended))
    col_out = exchange(attended)
    out_pieces = along_x(rest[:, :, QKV:])
    row_out = row_heads(sequence, both_cores(row_pieces))
    out_pieces, row_out = lax.optimization_barrier((out_pieces, row_out))
    return project_out(row_out, col_out.reshape(STRIDE, HALF), both_cores(out_pieces))[None]


def solution(mesh):
    in_specs = (
        P("fsdp", "seq", None),
        P("fsdp", None),
        P("fsdp", None),
        P("fsdp", None),
        P("fsdp", None),
        P(),
    )
    out_specs = P("fsdp", "seq", None)
    return jax.shard_map(shards, mesh=mesh, in_specs=in_specs, out_specs=out_specs, check_vma=False)
```
